32 devices in a mesh: seq: 16 (over z, y, core), dp: 2 (over x).
Axes of the slice: x: 2, y: 2, z: 4, core: 2. Of those that a mesh axis runs over, the one named last changes fastest.
Arguments:
- xin: bfloat16 [4096, 4096], P(('dp', 'seq')), parts along dimension 0, may hold values from -6 to 6
- zgate: bfloat16 [4096, 4096], P(('dp', 'seq')), parts along dimension 0, may hold values from -6 to 6
- delta_raw: bfloat16 [4096, 4096], P(('dp', 'seq')), parts along dimension 0, may hold values from -6 to 6
- bmat: float32 [16, 4096], P(None, ('dp', 'seq')), parts along dimension 1, may hold values from -6 to 6
- cmat: float32 [16, 4096], P(None, ('dp', 'seq')), parts along dimension 1, may hold values from -6 to 6
- conv_w: float32 [4, 4096], replicated, may hold values from -3 to 3
- conv_b: float32 [4096], replicated, may hold values from -0.5 to 0.5
- decay_rate: float32 [16, 4096], replicated, may hold values from 0.00048828125 to 3
- dskip: float32 [4096], replicated, may hold values from 0.1 to 1.9
- dt_bias: float32 [4096], replicated, may hold values from -6 to -3
- grad_out: bfloat16 [4096, 4096], P(('dp', 'seq')), parts along dimension 0, may hold values from -6 to 6
Outputs:
- grad_x: bfloat16 [4096, 4096], P(('dp', 'seq')), parts along dimension 0
- grad_z: bfloat16 [4096, 4096], P(('dp', 'seq')), parts along dimension 0
- grad_delta: bfloat16 [4096, 4096], P(('dp', 'seq')), parts along dimension 0
- grad_b: float32 [16, 4096], P(None, ('dp', 'seq')), parts along dimension 1
- grad_c: float32 [16, 4096], P(None, ('dp', 'seq')), parts along dimension 1
- grad_convw: float32 [8, 4096], P('dp'), parts along dimension 0
- grad_convb: float32 [8192], P('dp'), parts along dimension 0
- grad_rate: float32 [32, 4096], P('dp'), parts along dimension 0
- grad_skip: float32 [8192], P('dp'), parts along dimension 0
- grad_dtbias: float32 [8192], P('dp'), parts along dimension 0
The draws below stay inside these ranges and needn't reach their ends.
There are 2 independent parts, one for each index of `dp`. The reference program is written for one: setup_inputs(seed, part) draws one part's arguments, and reference() takes and returns one part's arrays. A program takes and returns all parts, laid end to end along the dimension named above; an argument that names none is the same for every part. Nothing has to cross between parts.
All inputs are finite; a program needn't handle non-finite values.
Results may differ from the reference program's by a relative error of at most 0.001.
Values may be sent and summed in bfloat16 or wider, within the bound.
No kernel may reach another device: no remote copies, remote signals or barrier semaphores. Data moves between devices by JAX's collectives and lax.ppermute only.
A program may use at most 448 MiB of HBM per device.

```python
import math
import jax
import jax.numpy as jnp
from jax import lax

ECH = 4096
STATE = 16
KCONV = 4
TOK_DEV = 128
SEQLEN = 2048


def level_of(key, dims, shards, smallest, high):
    loudness, own = 1.0, jax.random.fold_in(key, 6)
    for position, shards_of in shards:
        steps = jnp.exp(jax.random.uniform(jax.random.fold_in(own, position), (shards_of,), jnp.float32, smallest / len(shards), high / len(shards)))
        loudness = loudness * jnp.repeat(steps, dims[position] // shards_of).reshape([-1 if axis == position else 1 for axis in range(len(dims))])
    return loudness


def centred(stream_key, shape, scale, most, pieces=(), dtype=jnp.bfloat16):
    level = level_of(stream_key, shape, pieces, -0.22, 0.18) if pieces else 1.0
    result = jax.random.normal(stream_key, shape, jnp.float32) * scale * level
    return jnp.minimum(jnp.maximum(result, -most), most).astype(dtype)


def setup_inputs(seed: int = 0, part: int = 0) -> dict:
    seeds = jax.random.split(jax.random.key(seed), 12)
    own_keys = jax.random.split(jax.random.fold_in(seeds[11], part), 12)
    xin = centred(own_keys[0], (SEQLEN, ECH), 1.0, 6.0, ((0, 16),))
    zgate = centred(own_keys[1], (SEQLEN, ECH), 1.0, 6.0, ((0, 16),))
    delta_raw = centred(own_keys[2], (SEQLEN, ECH), 1.0, 6.0, ((0, 16),))
    bmat = centred(own_keys[3], (STATE, SEQLEN), 1.0, 6.0, ((1, 16),), jnp.float32)
    cmat = centred(own_keys[4], (STATE, SEQLEN), 1.0, 6.0, ((1, 16),), jnp.float32)
    conv_w = centred(seeds[5], (KCONV, ECH), KCONV ** -0.5, 3.0, (), jnp.float32)
    conv_b = jnp.clip(jax.random.uniform(seeds[6], (ECH,), jnp.float32, -0.5, 0.5), -0.5, 0.5)
    decay_rate = jnp.clip(jnp.exp(jax.random.uniform(seeds[7], (STATE, ECH), jnp.float32, math.log(0.00048828125), math.log(3.0))), 0.00048828125, 3.0)
    dskip = jnp.clip(1.0 + 0.18 * jax.random.normal(seeds[8], (ECH,), jnp.float32), 0.1, 1.9)
    dt_bias = jnp.clip(jax.random.uniform(seeds[9], (ECH,), jnp.float32, -6.0, -3.0), -6.0, -3.0)
    grad_out = centred(own_keys[10], (SEQLEN, ECH), 1.0, 6.0, ((0, 16),))
    return {"xin": xin, "zgate": zgate, "delta_raw": delta_raw, "bmat": bmat, "cmat": cmat, "conv_w": conv_w, "conv_b": conv_b, "decay_rate": decay_rate, "dskip": dskip, "dt_bias": dt_bias, "grad_out": grad_out}


def combine(first, second):
    return (first[0] * second[0], second[0] * first[1] + second[1])


def local_forward(delta, inner, bcol, rate):
    decay = jnp.exp(-delta[:, None, :] * rate[None, :, :])
    driven = (delta * inner)[:, None, :] * bcol[:, :, None]
    acum, hloc = lax.associative_scan(combine, (decay, driven), axis=0)
    return decay, acum, hloc


def local_reverse(decay, gy, ccol):
    source = gy[:, None, :] * ccol[:, :, None]
    mult = jnp.concatenate([decay[1:], jnp.ones_like(decay[:1])], axis=0)
    mflip, xflip = lax.associative_scan(combine, (mult[::-1], source[::-1]), axis=0)
    return mflip[::-1], xflip[::-1]


def local_grads(delta, inner, gy, bcol, ccol, rate, state_in, carry_back):
    hp = lax.Precision.HIGHEST
    decay, acum, hloc = local_forward(delta, inner, bcol, rate)
    state = hloc + acum * state_in[None]
    mcum, xloc = local_reverse(decay, gy, ccol)
    adj = xloc + mcum * carry_back[None]
    hprev = jnp.concatenate([state_in[None], state[:-1]], axis=0)
    ahp = decay * hprev
    yscan = jnp.einsum('tn,tne->te', ccol, state, precision=hp)
    gbsum = jnp.einsum('tne,tn->te', adj, bcol, precision=hp)
    gah = adj * ahp
    ddt = gbsum * inner - jnp.einsum('tne,ne->te', gah, rate, precision=hp)
    drate = -jnp.einsum('tne,te->ne', gah, delta, precision=hp)
    dbpart = jnp.einsum('tne,te->nt', adj, delta * inner, precision=hp)
    dcpart = jnp.einsum('te,tne->nt', gy, state, precision=hp)
    return yscan, ddt, gbsum * delta, dbpart, dcpart, drate


def reference(xin, zgate, delta_raw, bmat, cmat, conv_w, conv_b, decay_rate, dskip, dt_bias, grad_out):
    total, width = xin.shape
    blocks = total // TOK_DEV
    nstate = bmat.shape[0]
    xf = xin.astype(jnp.float32)
    xpad = jnp.pad(xf, ((KCONV - 1, 0), (0, 0)))
    conv = conv_b[None, :] + sum(conv_w[k][None, :] * xpad[k:k + total] for k in range(KCONV))
    sig_c = jax.nn.sigmoid(conv)
    inner = conv * sig_c
    dtin = delta_raw.astype(jnp.float32) + dt_bias[None, :]
    delta = jax.nn.softplus(dtin)
    zf = zgate.astype(jnp.float32)
    sig_z = jax.nn.sigmoid(zf)
    gof = grad_out.astype(jnp.float32)
    gy = gof * zf * sig_z
    dblk = delta.reshape(blocks, TOK_DEV, width)
    ublk = inner.reshape(blocks, TOK_DEV, width)
    gblk = gy.reshape(blocks, TOK_DEV, width)
    bblk = bmat.T.reshape(blocks, TOK_DEV, nstate)
    cblk = cmat.T.reshape(blocks, TOK_DEV, nstate)

    def fwd_step(carry, item):
        dpart, upart, bpart = item
        decay, acum, hloc = local_forward(dpart, upart, bpart, decay_rate)
        return acum[-1] * carry + hloc[-1], carry

    zero_state = jnp.zeros((nstate, width), jnp.float32)
    _, state_ins = lax.scan(fwd_step, zero_state, (dblk, ublk, bblk))

    def rev_step(carry, item):
        dpart, upart, gpart, bpart, cpart = item
        decay, acum, hloc = local_forward(dpart, upart, bpart, decay_rate)
        mcum, xloc = local_reverse(decay, gpart, cpart)
        return decay[0] * (xloc[0] + mcum[0] * carry), carry

    _, backs = lax.scan(rev_step, zero_state, (dblk, ublk, gblk, bblk, cblk), reverse=True)

    def third(item):
        dpart, upart, gpart, bpart, cpart, sin, rin = item
        return local_grads(dpart, upart, gpart, bpart, cpart, decay_rate, sin, rin)

    yscan, ddt, duscan, dbp, dcp, drates = lax.map(third, (dblk, ublk, gblk, bblk, cblk, state_ins, backs))
    yscan = yscan.reshape(total, width)
    ddt = ddt.reshape(total, width)
    duscan = duscan.reshape(total, width)
    grad_b = jnp.transpose(dbp, (1, 0, 2)).reshape(nstate, total)
    grad_c = jnp.transpose(dcp, (1, 0, 2)).reshape(nstate, total)
    grad_rate = jnp.sum(drates, axis=0)
    yfull = yscan + dskip[None, :] * inner
    grad_skip = jnp.sum(gy * inner, axis=0)
    dinner = duscan + gy * dskip[None, :]
    grad_z = (gof * yfull * sig_z * (1.0 + zf * (1.0 - sig_z))).astype(jnp.bfloat16)
    dd = ddt * jax.nn.sigmoid(dtin)
    grad_dtbias = jnp.sum(dd, axis=0)
    grad_delta = dd.astype(jnp.bfloat16)
    dcv = dinner * sig_c * (1.0 + conv * (1.0 - sig_c))
    grad_convb = jnp.sum(dcv, axis=0)
    grad_convw = jnp.stack([jnp.sum(dcv * xpad[k:k + total], axis=0) for k in range(KCONV)])
    dcpad = jnp.pad(dcv, ((0, KCONV - 1), (0, 0)))
    grad_x = sum(conv_w[k][None, :] * dcpad[KCONV - 1 - k:KCONV - 1 - k + total] for k in range(KCONV))
    return (grad_x.astype(jnp.bfloat16), grad_z, grad_delta, grad_b, grad_c, grad_convw, grad_convb, grad_rate, grad_skip, grad_dtbias)
```

```python
import functools
import math

import jax
import jax.numpy as jnp
from jax import lax
from jax.experimental import pallas as pl
from jax.experimental.pallas import tpu as pltpu
from jax.sharding import PartitionSpec as P

LANE = 128
SUB = 8
LOG2E = math.log2(math.e)
VMEM_BYTES = 60 * 1024 * 1024


def tile_rows(start):
    return pl.ds(pl.multiple_of(start, SUB), SUB)


def spread(src, dst, blocks, base, scale=None):
    rows = src.shape[0]
    for blk in range(blocks):
        piece = src[:, blk * LANE : (blk + 1) * LANE].astype(jnp.float32)
        if scale is not None:
            piece = piece * scale
        dst[pl.ds(base + blk, rows, stride=blocks), :] = piece


def spread_tokens(src, dst, tokens, blocks, lead):
    def some(group, carry):
        first = pl.multiple_of(group * 16, 16)
        for blk in range(blocks):
            piece = src[pl.ds(first, 16), blk * LANE : (blk + 1) * LANE].astype(jnp.float32)
            dst[pl.ds((first + lead) * blocks + blk, 16, stride=blocks), :] = piece
        return carry

    lax.fori_loop(0, tokens // 16, some, 0)


def gather_tokens(src, dst, tokens, blocks, lead):
    def some(group, carry):
        first = pl.multiple_of(group * 16, 16)
        for blk in range(blocks):
            piece = src[pl.ds((first + lead) * blocks + blk, 16, stride=blocks), :]
            dst[pl.ds(first, 16), blk * LANE : (blk + 1) * LANE] = piece.astype(dst.dtype)
        return carry

    lax.fori_loop(0, tokens // 16, some, 0)


def splat_columns(src, dst, tokens):
    flipped = src[...].T
    for n in range(src.shape[0]):
        dst[pl.ds(n * tokens, tokens), :] = jnp.broadcast_to(flipped[:, n : n + 1], (tokens, LANE))


def splat(ref, row):
    return jnp.broadcast_to(ref[pl.ds(row, 1), :], (SUB, LANE))


def steps(total, unroll, body, carry):
    def several(group, carry):
        for k in range(unroll):
            carry = body(group * unroll + k, carry)
        return carry

    return lax.fori_loop(0, total // unroll, several, carry)


def sigmoid(value):
    return 1.0 / (1.0 + jnp.exp(-value))


def local_body(
    tokens, blocks, nstate, taps,
    x_ref, draw_ref, z_ref, go_ref, rim_ref, b_ref, c_ref, w_ref, cb_ref, dtb_ref, rate_ref,
    pay_ref,
    xs, dts, dus, gys, bs, cs, ws, nrates,
):
    lead = taps - 1
    parts = blocks // SUB
    spread_tokens(x_ref, xs, tokens, blocks, lead)
    xs[0 : lead * blocks, :] = rim_ref[...].astype(jnp.float32)
    spread_tokens(draw_ref, dts, tokens, blocks, 0)
    spread_tokens(z_ref, dus, tokens, blocks, 0)
    spread_tokens(go_ref, gys, tokens, blocks, 0)
    spread(w_ref, ws, blocks, 0)
    spread(rate_ref, nrates, blocks, 0, -LOG2E)
    splat_columns(b_ref, bs, tokens)
    splat_columns(c_ref, cs, tokens)

    for m in range(parts):
        taps_here = [ws[tile_rows(k * blocks + m * SUB), :] for k in range(taps)]
        cb = cb_ref[tile_rows(m * SUB), :]
        dtb = dtb_ref[tile_rows(m * SUB), :]

        def pre(t, total, m=m, taps_here=taps_here, cb=cb, dtb=dtb):
            here = tile_rows(t * blocks + m * SUB)
            conv = cb
            for k in range(taps):
                conv = conv + taps_here[k] * xs[tile_rows((t + k) * blocks + m * SUB), :]
            inner = conv * sigmoid(conv)
            delta = jnp.log1p(jnp.exp(dts[here, :] + dtb))
            zf = dus[here, :]
            gys[here, :] = gys[here, :] * zf * sigmoid(zf)
            dts[here, :] = delta
            dus[here, :] = delta * inner
            return total + delta

        total = steps(tokens, 4, pre, jnp.zeros((SUB, LANE), jnp.float32))
        width = pay_ref.shape[0] // blocks
        pay_ref[pl.ds(m * SUB * width + 2 * nstate, SUB, stride=width), :] = total

    width = pay_ref.shape[0] // blocks
    group = 2
    for first in range(0, nstate, group):
        rates = [
            [nrates[tile_rows((first + n) * blocks + m * SUB), :] for m in range(parts)]
            for n in range(group)
        ]

        def scan(t, carry, first=first, rates=rates):
            state, cum, pulled = carry
            delta = [dts[tile_rows(t * blocks + m * SUB), :] for m in range(parts)]
            driven = [dus[tile_rows(t * blocks + m * SUB), :] for m in range(parts)]
            gy = [gys[tile_rows(t * blocks + m * SUB), :] for m in range(parts)]
            state, cum, pulled = list(state), list(cum), list(pulled)
            for n in range(group):
                bb = splat(bs, (first + n) * tokens + t)
                cc = splat(cs, (first + n) * tokens + t)
                for m in range(parts):
                    at = n * parts + m
                    decay = jnp.exp2(delta[m] * rates[n][m])
                    state[at] = decay * state[at] + driven[m] * bb
                    cum[at] = cum[at] * decay
                    pulled[at] = pulled[at] + cum[at] * (gy[m] * cc)
            return tuple(state), tuple(cum), tuple(pulled)

        zero = jnp.zeros((SUB, LANE), jnp.float32)
        one = jnp.ones((SUB, LANE), jnp.float32)
        count = group * parts
        state, cum, pulled = steps(
            tokens, 4, scan, ((zero,) * count, (one,) * count, (zero,) * count)
        )
        for n in range(group):
            for m in range(parts):
                at = n * parts + m
                pay_ref[pl.ds(m * SUB * width + first + n, SUB, stride=width), :] = state[at]
                pay_ref[pl.ds(m * SUB * width + nstate + first + n, SUB, stride=width), :] = pulled[at]


def carry_body(count, mine, span, nstate, width, got_ref, rate_ref, out_ref):
    for blk in range(mine):
        rate = rate_ref[:, blk * span : (blk + 1) * span]
        state = jnp.zeros((nstate, span), jnp.float32)
        back = jnp.zeros((nstate, span), jnp.float32)
        for step in range(count):
            base, outs = (step * mine + blk) * width, (step * mine + blk) * 2 * nstate
            out_ref[outs : outs + nstate, :] = state
            keep = jnp.exp(-rate * got_ref[base + 2 * nstate : base + 2 * nstate + 1, :])
            state = keep * state + got_ref[base : base + nstate, :]
            run = count - 1 - step
            base, outs = (run * mine + blk) * width, (run * mine + blk) * 2 * nstate
            out_ref[outs + nstate : outs + 2 * nstate, :] = back
            keep = jnp.exp(-rate * got_ref[base + 2 * nstate : base + 2 * nstate + 1, :])
            back = keep * back + got_ref[base + nstate : base + 2 * nstate, :]


def grads_body(
    tokens, blocks, nstate, taps,
    x_ref, draw_ref, z_ref, go_ref, rim_ref, b_ref, c_ref, w_ref, cb_ref, dtb_ref, rate_ref,
    skip_ref, in_ref,
    gx_ref, gz_ref, gd_ref, gb_ref, gc_ref, owed_ref, par_ref,
    xs, dts, dus, us, gys, bs, cs, ws, rates_s, ys, gbs, dds, zfs, sls, hs, pcs, pbs,
):
    lead = taps - 1
    parts = blocks // SUB
    count = 2 * nstate
    spread_tokens(x_ref, xs, tokens, blocks, lead)
    xs[0 : lead * blocks, :] = rim_ref[...].astype(jnp.float32)
    spread_tokens(draw_ref, dts, tokens, blocks, 0)
    spread_tokens(z_ref, zfs, tokens, blocks, 0)
    spread_tokens(go_ref, gys, tokens, blocks, 0)
    spread(w_ref, ws, blocks, 0)
    spread(rate_ref, rates_s, blocks, 0)
    splat_columns(b_ref, bs, tokens)
    splat_columns(c_ref, cs, tokens)
    width = par_ref.shape[0] // blocks
    zero = jnp.zeros((SUB, LANE), jnp.float32)

    for m in range(parts):
        taps_here = [ws[tile_rows(k * blocks + m * SUB), :] for k in range(taps)]
        cb = cb_ref[tile_rows(m * SUB), :]
        dtb = dtb_ref[tile_rows(m * SUB), :]
        skip = skip_ref[tile_rows(m * SUB), :]

        def pre(t, total, m=m, taps_here=taps_here, cb=cb, dtb=dtb, skip=skip):
            here = tile_rows(t * blocks + m * SUB)
            conv = cb
            for k in range(taps):
                conv = conv + taps_here[k] * xs[tile_rows((t + k) * blocks + m * SUB), :]
            sig_c = sigmoid(conv)
            inner = conv * sig_c
            delta = jnp.log1p(jnp.exp(dts[here, :] + dtb))
            zf = zfs[here, :]
            sig_z = sigmoid(zf)
            gof = gys[here, :]
            gy = gof * zf * sig_z
            gys[here, :] = gy
            dts[here, :] = delta
            us[here, :] = inner
            dus[here, :] = delta * inner
            zfs[here, :] = gof * sig_z * (1.0 + zf * (1.0 - sig_z))
            sls[here, :] = sig_c * (1.0 + conv * (1.0 - sig_c))
            ys[here, :] = skip * inner
            gbs[here, :] = zero
            dds[here, :] = zero
            return total + gy * inner

        total = steps(tokens, 4, pre, zero)
        par_ref[pl.ds(m * SUB * width + nstate + taps + 1, SUB, stride=width), :] = total

    group = 4
    cells = group * parts
    for first in range(0, nstate, group):
        def nrate(n, m, first=first):
            return rates_s[tile_rows((first + n) * blocks + m * SUB), :]

        negs = [[-LOG2E * nrate(n, m) for m in range(parts)] for n in range(group)]
        state = tuple(
            in_ref[pl.ds(m * SUB * count + first + n, SUB, stride=count), :]
            for n in range(group)
            for m in range(parts)
        )
        for at in range(cells):
            hs[at * SUB : (at + 1) * SUB, :] = state[at]

        def forward(t, state, first=first, negs=negs):
            delta = [dts[tile_rows(t * blocks + m * SUB), :] for m in range(parts)]
            driven = [dus[tile_rows(t * blocks + m * SUB), :] for m in range(parts)]
            gy = [gys[tile_rows(t * blocks + m * SUB), :] for m in range(parts)]
            y = [ys[tile_rows(t * blocks + m * SUB), :] for m in range(parts)]
            state = list(state)
            for n in range(group):
                bb = splat(bs, (first + n) * tokens + t)
                cc = splat(cs, (first + n) * tokens + t)
                pulled = None
                for m in range(parts):
                    at = n * parts + m
                    decay = jnp.exp2(delta[m] * negs[n][m])
                    now = decay * state[at] + driven[m] * bb
                    state[at] = now
                    hs[tile_rows(((t + 1) * cells + at) * SUB), :] = now
                    y[m] = y[m] + cc * now
                    term = gy[m] * now
                    pulled = term if pulled is None else pulled + term
                pcs[tile_rows((n * tokens + t) * SUB), :] = pulled
            for m in range(parts):
                ys[tile_rows(t * blocks + m * SUB), :] = y[m]
            return tuple(state)

        steps(tokens, 2, forward, state)

        back = tuple(
            in_ref[pl.ds(m * SUB * count + nstate + first + n, SUB, stride=count), :]
            for n in range(group)
            for m in range(parts)
        )

        def backward(step, carry, first=first, nrate=nrate):
            t = tokens - 1 - step
            back, acc = carry
            back, acc = list(back), list(acc)
            delta = [dts[tile_rows(t * blocks + m * SUB), :] for m in range(parts)]
            driven = [dus[tile_rows(t * blocks + m * SUB), :] for m in range(parts)]
            gy = [gys[tile_rows(t * blocks + m * SUB), :] for m in range(parts)]
            gsum = [gbs[tile_rows(t * blocks + m * SUB), :] for m in range(parts)]
            dsum = [dds[tile_rows(t * blocks + m * SUB), :] for m in range(parts)]
            for n in range(group):
                bb = splat(bs, (first + n) * tokens + t)
                cc = splat(cs, (first + n) * tokens + t)
                pulled = None
                for m in range(parts):
                    at = n * parts + m
                    rate = nrate(n, m)
                    scaled = delta[m] * rate
                    decay = jnp.exp2(scaled * -LOG2E)
                    adj = gy[m] * cc + back[at]
                    gsum[m] = gsum[m] + adj * bb
                    pushed = decay * adj
                    back[at] = pushed
                    gah = pushed * hs[tile_rows((t * cells + at) * SUB), :]
                    dsum[m] = dsum[m] + gah * rate
                    acc[at] = acc[at] - gah * delta[m]
                    term = adj * driven[m]
                    pulled = term if pulled is None else pulled + term
                pbs[tile_rows((n * tokens + t) * SUB), :] = pulled
            for m in range(parts):
                gbs[tile_rows(t * blocks + m * SUB), :] = gsum[m]
                dds[tile_rows(t * blocks + m * SUB), :] = dsum[m]
            return tuple(back), tuple(acc)

        _, acc = steps(tokens, 2, backward, (back, (zero,) * cells))
        for n in range(group):
            for m in range(parts):
                at = n * parts + m
                par_ref[pl.ds(m * SUB * width + first + n, SUB, stride=width), :] = acc[at]

        ones = jnp.ones((SUB, LANE), jnp.float32)
        for sums, out in ((pcs, gc_ref), (pbs, gb_ref)):
            for n in range(group):
                rows = sums[pl.ds(n * tokens * SUB, tokens, stride=SUB), :]
                for s in range(1, SUB):
                    rows = rows + sums[pl.ds(n * tokens * SUB + s, tokens, stride=SUB), :]
                line = lax.dot_general(
                    ones, rows, (((1,), (1,)), ((), ())),
                    precision=lax.Precision.HIGHEST, preferred_element_type=jnp.float32,
                )
                out[first + n : first + n + 1, :] = line[0:1, :]

    for m in range(parts):
        dtb = dtb_ref[tile_rows(m * SUB), :]
        skip = skip_ref[tile_rows(m * SUB), :]

        def post(t, carry, m=m, dtb=dtb, skip=skip):
            bias, convb, convw = carry
            here = tile_rows(t * blocks + m * SUB)
            delta, inner, gy = dts[here, :], us[here, :], gys[here, :]
            gsum = gbs[here, :]
            ddt = gsum * inner - dds[here, :]
            dd = ddt * dus[here, :]
            dcv = (gsum * delta + gy * skip) * sls[here, :]
            dds[here, :] = dd
            gbs[here, :] = dcv
            zfs[here, :] = zfs[here, :] * ys[here, :]
            convw = tuple(
                convw[k] + dcv * xs[tile_rows((t + k) * blocks + m * SUB), :] for k in range(taps)
            )
            return bias + dd, convb + dcv, convw

        def refill(t, carry, m=m, dtb=dtb):
            here = tile_rows(t * blocks + m * SUB)
            grow = jnp.exp(dus[here, :] + dtb)
            dus[here, :] = grow / (1.0 + grow)
            return carry

        if m == 0:
            spread_tokens(draw_ref, dus, tokens, blocks, 0)
        steps(tokens, 4, refill, 0)
        bias, convb, convw = steps(tokens, 2, post, (zero, zero, (zero,) * taps))
        for row, value in zip(
            [nstate + k for k in range(taps)] + [nstate + taps, nstate + taps + 2],
            list(convw) + [convb, bias],
        ):
            par_ref[pl.ds(m * SUB * width + row, SUB, stride=width), :] = value
        taps_here = [ws[tile_rows(k * blocks + m * SUB), :] for k in range(taps)]

        def spill(t, carry, m=m, taps_here=taps_here):
            value = taps_here[0] * gbs[tile_rows((t + lead) * blocks + m * SUB), :]
            for k in range(1, taps):
                value = value + taps_here[k] * gbs[tile_rows((t + lead - k) * blocks + m * SUB), :]
            ys[tile_rows(t * blocks + m * SUB), :] = value
            return carry

        lax.fori_loop(0, tokens - lead, spill, 0)
        for s in range(tokens - lead, tokens):
            value = zero
            for k in range(taps):
                if s + lead - k < tokens:
                    value = value + taps_here[k] * gbs[tile_rows((s + lead - k) * blocks + m * SUB), :]
            ys[tile_rows(s * blocks + m * SUB), :] = value
            owed_ref[tile_rows((s - tokens + lead + lead) * blocks + m * SUB), :] = value
        for s in range(lead):
            value = zero
            for k in range(taps):
                if s - k >= 0:
                    value = value + taps_here[k] * gbs[tile_rows((s - k) * blocks + m * SUB), :]
            owed_ref[tile_rows(s * blocks + m * SUB), :] = value

    gather_tokens(ys, gx_ref, tokens, blocks, 0)
    gather_tokens(zfs, gz_ref, tokens, blocks, 0)
    gather_tokens(dds, gd_ref, tokens, blocks, 0)


def whole(count):
    return [pl.BlockSpec(memory_space=pltpu.VMEM)] * count


def slices(rows, runs):
    blocks, width, lanes = rows.shape
    if blocks % runs == 0:
        return rows.reshape(runs, blocks // runs * width, lanes)
    narrow = blocks * lanes // runs
    return rows.transpose(1, 0, 2).reshape(width, runs, narrow).transpose(1, 0, 2)


def unslices(pieces, blocks, width):
    runs = pieces.shape[0]
    if blocks % runs == 0:
        return pieces.reshape(blocks, width, LANE)
    return pieces.transpose(1, 0, 2).reshape(width, blocks, LANE).transpose(1, 0, 2)


def swap(pieces):
    return lax.all_to_all(pieces, "seq", 0, 0, tiled=True)


def shards(xin, zgate, delta_raw, bmat, cmat, conv_w, conv_b, decay_rate, dskip, dt_bias, grad_out):
    tokens, channels = xin.shape
    nstate, taps = bmat.shape[0], conv_w.shape[0]
    lead = taps - 1
    blocks = channels // LANE
    runs = lax.axis_size("seq")
    me = lax.axis_index("seq")
    mine = max(1, blocks // runs)
    span = channels // runs // mine
    vec = lambda rows: pltpu.VMEM((rows, LANE), jnp.float32)
    f32 = lambda *shape: jax.ShapeDtypeStruct(shape, jnp.float32)
    params = pltpu.CompilerParams(vmem_limit_bytes=VMEM_BYTES)

    rim = lax.ppermute(
        xin[tokens - lead :].reshape(lead * blocks, LANE), "seq",
        [(i, i + 1) for i in range(runs - 1)],
    )
    cb, dtb, skip = (v.reshape(blocks, LANE) for v in (conv_b, dt_bias, dskip))
    full = tokens * blocks
    width = 2 * nstate + SUB
    pay = pl.pallas_call(
        functools.partial(local_body, tokens, blocks, nstate, taps),
        out_shape=f32(blocks * width, LANE),
        in_specs=whole(11),
        out_specs=whole(1)[0],
        scratch_shapes=[
            vec(full + lead * blocks), vec(full), vec(full), vec(full),
            vec(nstate * tokens), vec(nstate * tokens), vec(taps * blocks), vec(nstate * blocks),
        ],
        compiler_params=params,
        name="local_scan",
    )(xin, delta_raw, zgate, grad_out, rim, bmat, cmat, conv_w, cb, dtb, decay_rate)
    got = swap(slices(pay.reshape(blocks, width, LANE), runs))
    rate_mine = lax.dynamic_slice(decay_rate, (0, me * mine * span), (nstate, mine * span))
    carries = pl.pallas_call(
        functools.partial(carry_body, runs, mine, span, nstate, width),
        out_shape=f32(runs * mine * 2 * nstate, span),
        in_specs=whole(2),
        out_specs=whole(1)[0],
        compiler_params=params,
        name="carry_scan",
    )(got.reshape(runs * mine * width, span), rate_mine)
    ins = unslices(swap(carries.reshape(runs, mine * 2 * nstate, span)), blocks, 2 * nstate)
    rows = nstate + taps + 4
    rows = rows + (-rows) % SUB
    bf = lambda *shape: jax.ShapeDtypeStruct(shape, jnp.bfloat16)
    gx, gz, gd, gb, gc, owed, par = pl.pallas_call(
        functools.partial(grads_body, tokens, blocks, nstate, taps),
        out_shape=(
            bf(tokens, channels), bf(tokens, channels), bf(tokens, channels),
            f32(nstate, tokens), f32(nstate, tokens),
            f32(2 * lead * blocks, LANE), f32(blocks * rows, LANE),
        ),
        in_specs=whole(13),
        out_specs=tuple(whole(7)),
        scratch_shapes=[
            vec(full + lead * blocks), vec(full), vec(full), vec(full), vec(full),
            vec(nstate * tokens), vec(nstate * tokens), vec(taps * blocks), vec(nstate * blocks),
            vec(full), vec(full), vec(full), vec(full), vec(full),
            vec((tokens + 1) * 4 * blocks), vec(4 * tokens * SUB), vec(4 * tokens * SUB),
        ],
        compiler_params=params,
        name="grads",
    )(xin, delta_raw, zgate, grad_out, rim, bmat, cmat, conv_w, cb, dtb, decay_rate, skip,
      ins.reshape(blocks * 2 * nstate, LANE))
    returned = lax.ppermute(
        owed[: lead * blocks], "seq", [(i + 1, i) for i in range(runs - 1)]
    )
    last = (owed[lead * blocks :] + returned).reshape(lead, channels).astype(jnp.bfloat16)
    gx = lax.dynamic_update_slice(gx, last, (tokens - lead, 0))
    sums = jnp.sum(swap(slices(par.reshape(blocks, rows, LANE), runs)), axis=0)
    every = unslices(swap(jnp.broadcast_to(sums[None], (runs,) + sums.shape)), blocks, rows)
    flat = lambda a, b: every[:, a:b].transpose(1, 0, 2).reshape(b - a, channels)
    return (
        gx, gz, gd, gb, gc,
        flat(nstate, nstate + taps),
        every[:, nstate + taps].reshape(channels),
        flat(0, nstate),
        every[:, nstate + taps + 1].reshape(channels),
        every[:, nstate + taps + 2].reshape(channels),
    )


def solution(mesh):
    both = P(("dp", "seq"), None)
    across = P(None, ("dp", "seq"))
    return jax.shard_map(
        shards,
        mesh=mesh,
        in_specs=(both, both, both, across, across, P(), P(), P(), P(), P(), both),
        out_specs=(
            both, both, both, across, across,
            P("dp", None), P("dp"), P("dp", None), P("dp"), P("dp"),
        ),
        check_vma=False,
    )
```

```python
import functools
import math

import jax
import jax.numpy as jnp
from jax import lax
from jax.experimental import pallas as pl
from jax.experimental.pallas import tpu as pltpu
from jax.sharding import PartitionSpec as P

LANE = 128
SUB = 8
LOG2E = math.log2(math.e)
VMEM_BYTES = 60 * 1024 * 1024


def tile(start):
    return pl.ds(pl.multiple_of(start, SUB), SUB)


def spread_rows(src, dst, scale=None):
    rows, channels = src.shape
    blocks = channels // LANE
    for blk in range(blocks):
        piece = src[:, blk * LANE : (blk + 1) * LANE]
        dst[pl.ds(blk, rows, stride=blocks), :] = piece if scale is None else piece * scale


def spread_tokens(src, dst, lead=0):
    tokens, channels = src.shape
    blocks = channels // LANE
    plane = dst.shape[0] // (blocks // SUB)

    def some(group, carry):
        first = pl.multiple_of(group * 16, 16)
        for blk in range(blocks):
            piece = src[pl.ds(first, 16), blk * LANE : (blk + 1) * LANE].astype(jnp.float32)
            start = blk // SUB * plane + blk % SUB + (first + lead) * SUB
            dst[pl.ds(start, 16, stride=SUB), :] = piece
        return carry

    lax.fori_loop(0, tokens // 16, some, 0)


def gather_tokens(src, dst):
    tokens, channels = dst.shape
    blocks = channels // LANE
    plane = src.shape[0] // (blocks // SUB)

    def some(group, carry):
        first = pl.multiple_of(group * 16, 16)
        for blk in range(blocks):
            start = blk // SUB * plane + blk % SUB + first * SUB
            piece = src[pl.ds(start, 16, stride=SUB), :]
            dst[pl.ds(first, 16), blk * LANE : (blk + 1) * LANE] = piece.astype(dst.dtype)
        return carry

    lax.fori_loop(0, tokens // 16, some, 0)


def place_rim(rim_ref, xs, lead, parts):
    plane = xs.shape[0] // parts
    for r in range(lead):
        for m in range(parts):
            rows = rim_ref[(r * parts + m) * SUB : (r * parts + m + 1) * SUB, :]
            xs[m * plane + r * SUB : m * plane + (r + 1) * SUB, :] = rows.astype(jnp.float32)


def splat_columns(src, dst, tokens):
    flipped = src[...].T
    for n in range(src.shape[0]):
        dst[pl.ds(n * tokens, tokens), :] = jnp.broadcast_to(flipped[:, n : n + 1], (tokens, LANE))


def splat(ref, row):
    return jnp.broadcast_to(ref[pl.ds(row, 1), :], (SUB, LANE))


def steps(total, unroll, body, carry):
    def several(group, carry):
        for k in range(unroll):
            carry = body(group * unroll + k, carry)
        return carry

    return lax.fori_loop(0, total // unroll, several, carry)


def sigmoid(value):
    return 1.0 / (1.0 + jnp.exp(-value))


def conv_at(xs, ws, cb, m, t, taps, parts):
    plane = xs.shape[0] // parts
    conv = cb
    for k in range(taps):
        conv = conv + ws[k] * xs[tile(m * plane + (t + k) * SUB), :]
    return conv


GROUP = 2


def local_body(
    tokens, blocks, nstate, taps,
    x_ref, draw_ref, z_ref, go_ref, rim_ref, b_ref, c_ref, w_ref, cb_ref, dtb_ref, rate_ref,
    pay_ref,
    xs, dts, dus, gys, bs, cs, ws, nrates,
):
    parts = blocks // SUB
    plane = tokens * SUB
    width = pay_ref.shape[0] // blocks
    spread_tokens(x_ref, xs, taps - 1)
    place_rim(rim_ref, xs, taps - 1, parts)
    spread_tokens(draw_ref, dts)
    spread_tokens(z_ref, dus)
    spread_tokens(go_ref, gys)
    spread_rows(w_ref, ws)
    spread_rows(rate_ref, nrates, -LOG2E)
    splat_columns(b_ref, bs, tokens)
    splat_columns(c_ref, cs, tokens)
    zero = jnp.zeros((SUB, LANE), jnp.float32)
    one = jnp.ones((SUB, LANE), jnp.float32)

    for m in range(parts):
        taps_here = [ws[(k * parts + m) * SUB : (k * parts + m + 1) * SUB, :] for k in range(taps)]
        cb = cb_ref[m * SUB : (m + 1) * SUB, :]
        dtb = dtb_ref[m * SUB : (m + 1) * SUB, :]

        def pre(t, total, m=m, taps_here=taps_here, cb=cb, dtb=dtb):
            here = tile(m * plane + t * SUB)
            conv = conv_at(xs, taps_here, cb, m, t, taps, parts)
            inner = conv * sigmoid(conv)
            delta = jnp.log1p(jnp.exp(dts[here, :] + dtb))
            zf = dus[here, :]
            gys[here, :] = gys[here, :] * zf * sigmoid(zf)
            dts[here, :] = delta
            dus[here, :] = delta * inner
            return total + delta

        total = steps(tokens, 8, pre, zero)
        pay_ref[pl.ds(m * SUB * width + 2 * nstate, SUB, stride=width), :] = total

    def some(group, carry):
        first = group * GROUP
        rates = [
            nrates[tile(((first + n) * parts + m) * SUB), :]
            for n in range(GROUP) for m in range(parts)
        ]

        def scan(t, carry):
            state, cum, pulled = (list(part) for part in carry)
            delta, driven, gy = (
                [ref[tile(m * plane + t * SUB), :] for m in range(parts)] for ref in (dts, dus, gys)
            )
            for n in range(GROUP):
                bb = splat(bs, (first + n) * tokens + t)
                cc = splat(cs, (first + n) * tokens + t)
                for m in range(parts):
                    at = n * parts + m
                    decay = jnp.exp2(delta[m] * rates[at])
                    state[at] = decay * state[at] + driven[m] * bb
                    cum[at] = cum[at] * decay
                    pulled[at] = pulled[at] + cum[at] * (gy[m] * cc)
            return tuple(state), tuple(cum), tuple(pulled)

        count = GROUP * parts
        state, _, pulled = steps(
            tokens, 4, scan, ((zero,) * count, (one,) * count, (zero,) * count)
        )
        for n in range(GROUP):
            for m in range(parts):
                at = n * parts + m
                base = m * SUB * width + first + n
                pay_ref[pl.ds(base, SUB, stride=width), :] = state[at]
                pay_ref[pl.ds(base + nstate, SUB, stride=width), :] = pulled[at]
        return carry

    lax.fori_loop(0, nstate // GROUP, some, 0)


def carry_body(count, mine, span, nstate, width, got_ref, rate_ref, out_ref):
    for blk in range(mine):
        rate = rate_ref[:, blk * span : (blk + 1) * span]
        state = jnp.zeros((nstate, span), jnp.float32)
        back = jnp.zeros((nstate, span), jnp.float32)
        for step in range(count):
            base, outs = (step * mine + blk) * width, (step * mine + blk) * 2 * nstate
            out_ref[outs : outs + nstate, :] = state
            keep = jnp.exp(-rate * got_ref[base + 2 * nstate : base + 2 * nstate + 1, :])
            state = keep * state + got_ref[base : base + nstate, :]
            run = count - 1 - step
            base, outs = (run * mine + blk) * width, (run * mine + blk) * 2 * nstate
            out_ref[outs + nstate : outs + 2 * nstate, :] = back
            keep = jnp.exp(-rate * got_ref[base + 2 * nstate : base + 2 * nstate + 1, :])
            back = keep * back + got_ref[base + nstate : base + 2 * nstate, :]


def grads_body(
    tokens, blocks, nstate, taps,
    x_ref, draw_ref, z_ref, go_ref, rim_ref, b_ref, c_ref, w_ref, cb_ref, dtb_ref, rate_ref,
    skip_ref, in_ref,
    gx_ref, gz_ref, gd_ref, gb_ref, gc_ref, owed_ref, par_ref,
    xs, dts, dus, us, gys, bs, cs, ws, nrates, ys, gbs, dds, zfs, sls, sds, hs, pcs, pbs,
):
    lead = taps - 1
    parts = blocks // SUB
    plane = tokens * SUB
    count = in_ref.shape[0] // blocks
    width = par_ref.shape[0] // blocks
    spread_tokens(x_ref, xs, lead)
    place_rim(rim_ref, xs, lead, parts)
    spread_tokens(draw_ref, dts)
    spread_tokens(z_ref, zfs)
    spread_tokens(go_ref, gys)
    spread_rows(w_ref, ws)
    spread_rows(rate_ref, nrates, -LOG2E)
    splat_columns(b_ref, bs, tokens)
    splat_columns(c_ref, cs, tokens)
    zero = jnp.zeros((SUB, LANE), jnp.float32)

    def taps_of(m):
        return [ws[(k * parts + m) * SUB : (k * parts + m + 1) * SUB, :] for k in range(taps)]

    for m in range(parts):
        taps_here = taps_of(m)
        cb = cb_ref[m * SUB : (m + 1) * SUB, :]
        dtb = dtb_ref[m * SUB : (m + 1) * SUB, :]
        skip = skip_ref[m * SUB : (m + 1) * SUB, :]

        def pre(t, total, m=m, taps_here=taps_here, cb=cb, dtb=dtb, skip=skip):
            here = tile(m * plane + t * SUB)
            conv = conv_at(xs, taps_here, cb, m, t, taps, parts)
            sig_c = sigmoid(conv)
            inner = conv * sig_c
            grow = jnp.exp(dts[here, :] + dtb)
            delta = jnp.log1p(grow)
            zf = zfs[here, :]
            sig_z = sigmoid(zf)
            gof = gys[here, :] * sig_z
            gy = gof * zf
            gys[here, :] = gy
            dts[here, :] = delta
            us[here, :] = inner
            dus[here, :] = delta * inner
            zfs[here, :] = gof * (1.0 + zf * (1.0 - sig_z))
            sls[here, :] = sig_c * (1.0 + conv * (1.0 - sig_c))
            sds[here, :] = grow / (1.0 + grow)
            ys[here, :] = skip * inner
            gbs[here, :] = zero
            dds[here, :] = zero
            return total + gy * inner

        total = steps(tokens, 8, pre, zero)
        par_ref[pl.ds(m * SUB * width + nstate + taps + 1, SUB, stride=width), :] = total

    cells = GROUP * parts

    def some(group, carry):
        first = group * GROUP
        rates = [
            nrates[tile(((first + n) * parts + m) * SUB), :]
            for n in range(GROUP) for m in range(parts)
        ]

        def carried(offset):
            return tuple(
                in_ref[pl.ds(m * SUB * count + offset + first + n, SUB, stride=count), :]
                for n in range(GROUP) for m in range(parts)
            )

        state = carried(0)
        for at in range(cells):
            hs[at * SUB : (at + 1) * SUB, :] = state[at]

        def forward(t, state):
            state = list(state)
            delta, driven, gy, y = (
                [ref[tile(m * plane + t * SUB), :] for m in range(parts)]
                for ref in (dts, dus, gys, ys)
            )
            for n in range(GROUP):
                bb = splat(bs, (first + n) * tokens + t)
                cc = splat(cs, (first + n) * tokens + t)
                pulled = None
                for m in range(parts):
                    at = n * parts + m
                    decay = jnp.exp2(delta[m] * rates[at])
                    now = decay * state[at] + driven[m] * bb
                    state[at] = now
                    hs[tile(((t + 1) * cells + at) * SUB), :] = now
                    y[m] = y[m] + cc * now
                    term = gy[m] * now
                    pulled = term if pulled is None else pulled + term
                pcs[tile((n * tokens + t) * SUB), :] = pulled
            for m in range(parts):
                ys[tile(m * plane + t * SUB), :] = y[m]
            return tuple(state)

        steps(tokens, 4, forward, state)

        def backward(step, carry):
            t = tokens - 1 - step
            back, acc = (list(part) for part in carry)
            delta, driven, gy, gsum, dsum = (
                [ref[tile(m * plane + t * SUB), :] for m in range(parts)]
                for ref in (dts, dus, gys, gbs, dds)
            )
            for n in range(GROUP):
                bb = splat(bs, (first + n) * tokens + t)
                cc = splat(cs, (first + n) * tokens + t)
                pulled = None
                for m in range(parts):
                    at = n * parts + m
                    decay = jnp.exp2(delta[m] * rates[at])
                    adj = gy[m] * cc + back[at]
                    gsum[m] = gsum[m] + adj * bb
                    back[at] = decay * adj
                    gah = back[at] * hs[tile((t * cells + at) * SUB), :]
                    dsum[m] = dsum[m] + gah * rates[at]
                    acc[at] = acc[at] + gah * delta[m]
                    term = adj * driven[m]
                    pulled = term if pulled is None else pulled + term
                pbs[tile((n * tokens + t) * SUB), :] = pulled
            for m in range(parts):
                gbs[tile(m * plane + t * SUB), :] = gsum[m]
                dds[tile(m * plane + t * SUB), :] = dsum[m]
            return tuple(back), tuple(acc)

        _, acc = steps(tokens, 2, backward, (carried(nstate), (zero,) * cells))
        for n in range(GROUP):
            for m in range(parts):
                base = m * SUB * width + first + n
                par_ref[pl.ds(base, SUB, stride=width), :] = -acc[n * parts + m]

        def fold(piece, carry):
            for sums, out in ((pcs, gc_ref), (pbs, gb_ref)):
                rows = sums[pl.ds(piece * 32 * SUB, 32, stride=SUB), :]
                for s in range(1, SUB):
                    rows = rows + sums[pl.ds(piece * 32 * SUB + s, 32, stride=SUB), :]
                out[pl.ds(pl.multiple_of(first * tokens + piece * 32, 32), 32), :] = rows
            return carry

        lax.fori_loop(0, GROUP * tokens // 32, fold, 0)
        return carry

    lax.fori_loop(0, nstate // GROUP, some, 0)

    for m in range(parts):
        taps_here = taps_of(m)
        skip = skip_ref[m * SUB : (m + 1) * SUB, :]
        xplane = xs.shape[0] // parts

        def post(t, carry, m=m, skip=skip):
            bias, convb, convw = carry
            here = tile(m * plane + t * SUB)
            gsum = gbs[here, :]
            dd = (gsum * us[here, :] + dds[here, :] * (1.0 / LOG2E)) * sds[here, :]
            dcv = (gsum * dts[here, :] + gys[here, :] * skip) * sls[here, :]
            dds[here, :] = dd
            gbs[here, :] = dcv
            zfs[here, :] = zfs[here, :] * ys[here, :]
            convw = tuple(
                convw[k] + dcv * xs[tile(m * xplane + (t + k) * SUB), :] for k in range(taps)
            )
            return bias + dd, convb + dcv, convw

        bias, convb, convw = steps(tokens, 4, post, (zero, zero, (zero,) * taps))
        rows = [nstate + k for k in range(taps)] + [nstate + taps, nstate + taps + 2]
        for row, value in zip(rows, list(convw) + [convb, bias]):
            par_ref[pl.ds(m * SUB * width + row, SUB, stride=width), :] = value

        def spill(t, carry, m=m, taps_here=taps_here):
            value = None
            for k in range(taps):
                term = taps_here[k] * gbs[tile(m * plane + (t + lead - k) * SUB), :]
                value = term if value is None else value + term
            ys[tile(m * plane + t * SUB), :] = value
            return carry

        whole_steps = (tokens - lead) // 8 * 8
        steps(whole_steps, 8, spill, 0)
        for t in range(whole_steps, tokens - lead):
            spill(t, 0)

        def partial(s):
            value = zero
            for k in range(taps):
                if 0 <= s + lead - k < tokens:
                    value = value + taps_here[k] * gbs[tile(m * plane + (s + lead - k) * SUB), :]
            return value

        for i in range(lead):
            value = partial(tokens - lead + i)
            ys[tile(m * plane + (tokens - lead + i) * SUB), :] = value
            owed_ref[tile(((lead + i) * parts + m) * SUB), :] = value
            owed_ref[tile((i * parts + m) * SUB), :] = partial(i - lead)

    gather_tokens(ys, gx_ref)
    gather_tokens(zfs, gz_ref)
    gather_tokens(dds, gd_ref)


def whole(count):
    return [pl.BlockSpec(memory_space=pltpu.VMEM)] * count


def slices(rows, runs):
    blocks, width, lanes = rows.shape
    if blocks % runs == 0:
        return rows.reshape(runs, blocks // runs * width, lanes)
    narrow = blocks * lanes // runs
    return rows.transpose(1, 0, 2).reshape(width, runs, narrow).transpose(1, 0, 2)


def unslices(pieces, blocks, width):
    runs = pieces.shape[0]
    if blocks % runs == 0:
        return pieces.reshape(blocks, width, LANE)
    return pieces.transpose(1, 0, 2).reshape(width, blocks, LANE).transpose(1, 0, 2)


def swap(pieces):
    return lax.all_to_all(pieces, "seq", 0, 0, tiled=True)


def shards(xin, zgate, delta_raw, bmat, cmat, conv_w, conv_b, decay_rate, dskip, dt_bias, grad_out):
    tokens, channels = xin.shape
    nstate, taps = bmat.shape[0], conv_w.shape[0]
    lead = taps - 1
    blocks = channels // LANE
    runs = lax.axis_size("seq")
    me = lax.axis_index("seq")
    mine = max(1, blocks // runs)
    span = channels // runs // mine
    vec = lambda rows: pltpu.VMEM((rows, LANE), jnp.float32)
    f32 = lambda *shape: jax.ShapeDtypeStruct(shape, jnp.float32)
    params = pltpu.CompilerParams(vmem_limit_bytes=VMEM_BYTES)

    rim = lax.ppermute(
        xin[tokens - lead :].reshape(lead * blocks, LANE), "seq",
        [(i, i + 1) for i in range(runs - 1)],
    )
    cb, dtb, skip = (v.reshape(blocks, LANE) for v in (conv_b, dt_bias, dskip))
    full = tokens * blocks
    width = 2 * nstate + SUB
    pay = pl.pallas_call(
        functools.partial(local_body, tokens, blocks, nstate, taps),
        out_shape=f32(blocks * width, LANE),
        in_specs=whole(11),
        out_specs=whole(1)[0],
        scratch_shapes=[
            vec(full + lead * blocks), vec(full), vec(full), vec(full),
            vec(nstate * tokens), vec(nstate * tokens), vec(taps * blocks), vec(nstate * blocks),
        ],
        compiler_params=params,
        name="local_scan",
    )(xin, delta_raw, zgate, grad_out, rim, bmat, cmat, conv_w, cb, dtb, decay_rate)
    got = swap(slices(pay.reshape(blocks, width, LANE), runs))
    rate_mine = lax.dynamic_slice(decay_rate, (0, me * mine * span), (nstate, mine * span))
    carries = pl.pallas_call(
        functools.partial(carry_body, runs, mine, span, nstate, width),
        out_shape=f32(runs * mine * 2 * nstate, span),
        in_specs=whole(2),
        out_specs=whole(1)[0],
        compiler_params=params,
        name="carry_scan",
    )(got.reshape(runs * mine * width, span), rate_mine)
    ins = unslices(swap(carries.reshape(runs, mine * 2 * nstate, span)), blocks, 2 * nstate)
    rows = nstate + taps + 4
    rows = rows + (-rows) % SUB
    bf = lambda *shape: jax.ShapeDtypeStruct(shape, jnp.bfloat16)
    gx, gz, gd, gb, gc, owed, par = pl.pallas_call(
        functools.partial(grads_body, tokens, blocks, nstate, taps),
        out_shape=(
            bf(tokens, channels), bf(tokens, channels), bf(tokens, channels),
            f32(nstate * tokens, LANE), f32(nstate * tokens, LANE),
            f32(2 * lead * blocks, LANE), f32(blocks * rows, LANE),
        ),
        in_specs=whole(13),
        out_specs=tuple(whole(7)),
        scratch_shapes=[
            vec(full + lead * blocks), vec(full), vec(full), vec(full), vec(full),
            vec(nstate * tokens), vec(nstate * tokens), vec(taps * blocks), vec(nstate * blocks),
            vec(full), vec(full), vec(full), vec(full), vec(full), vec(full),
            vec((tokens + 1) * GROUP * blocks), vec(GROUP * tokens * SUB), vec(GROUP * tokens * SUB),
        ],
        compiler_params=params,
        name="grads",
    )(xin, delta_raw, zgate, grad_out, rim, bmat, cmat, conv_w, cb, dtb, decay_rate, skip,
      ins.reshape(blocks * 2 * nstate, LANE))
    gb, gc = (jnp.sum(v.reshape(nstate, tokens, LANE), axis=2) for v in (gb, gc))
    returned = lax.ppermute(
        owed[: lead * blocks], "seq", [(i + 1, i) for i in range(runs - 1)]
    )
    last = (owed[lead * blocks :] + returned).reshape(lead, channels).astype(jnp.bfloat16)
    gx = lax.dynamic_update_slice(gx, last, (tokens - lead, 0))
    sums = jnp.sum(swap(slices(par.reshape(blocks, rows, LANE), runs)), axis=0)
    every = unslices(swap(jnp.broadcast_to(sums[None], (runs,) + sums.shape)), blocks, rows)
    flat = lambda a, b: every[:, a:b].transpose(1, 0, 2).reshape(b - a, channels)
    return (
        gx, gz, gd, gb, gc,
        flat(nstate, nstate + taps),
        every[:, nstate + taps].reshape(channels),
        flat(0, nstate),
        every[:, nstate + taps + 1].reshape(channels),
        every[:, nstate + taps + 2].reshape(channels),
    )


def solution(mesh):
    both = P(("dp", "seq"), None)
    across = P(None, ("dp", "seq"))
    return jax.shard_map(
        shards,
        mesh=mesh,
        in_specs=(both, both, both, across, across, P(), P(), P(), P(), P(), both),
        out_specs=(
            both, both, both, across, across,
            P("dp", None), P("dp"), P("dp", None), P("dp"), P("dp"),
        ),
        check_vma=False,
    )
```

```python
import functools
import math

import jax
import jax.numpy as jnp
from jax import lax
from jax.experimental import pallas as pl
from jax.experimental.pallas import tpu as pltpu
from jax.sharding import PartitionSpec as P

LANE = 128
SUB = 8
LOG2E = math.log2(math.e)
LOCAL_MB, CARRY_MB, GRADS_MB = 20, 2, 30


def tile(start):
    return pl.ds(pl.multiple_of(start, SUB), SUB)


def spread_rows(src, dst, scale=None):
    rows, channels = src.shape
    blocks = channels // LANE
    for blk in range(blocks):
        piece = src[:, blk * LANE : (blk + 1) * LANE]
        dst[pl.ds(blk, rows, stride=blocks), :] = piece if scale is None else piece * scale


def spread_tokens(src, dst, lead=0):
    tokens, channels = src.shape
    blocks = channels // LANE
    plane = dst.shape[0] // (blocks // SUB)

    def some(group, carry):
        first = pl.multiple_of(group * 16, 16)
        for blk in range(blocks):
            piece = src[pl.ds(first, 16), blk * LANE : (blk + 1) * LANE].astype(jnp.float32)
            start = blk // SUB * plane + blk % SUB + (first + lead) * SUB
            dst[pl.ds(start, 16, stride=SUB), :] = piece
        return carry

    lax.fori_loop(0, tokens // 16, some, 0)


def gather_tokens(src, dst):
    tokens, channels = dst.shape
    blocks = channels // LANE
    plane = src.shape[0] // (blocks // SUB)

    def some(group, carry):
        first = pl.multiple_of(group * 16, 16)
        for blk in range(blocks):
            start = blk // SUB * plane + blk % SUB + first * SUB
            piece = src[pl.ds(start, 16, stride=SUB), :]
            dst[pl.ds(first, 16), blk * LANE : (blk + 1) * LANE] = piece.astype(dst.dtype)
        return carry

    lax.fori_loop(0, tokens // 16, some, 0)


def place_rim(rim_ref, xs, lead, parts):
    plane = xs.shape[0] // parts
    for r in range(lead):
        for m in range(parts):
            rows = rim_ref[r, m * SUB : (m + 1) * SUB, :]
            xs[m * plane + r * SUB : m * plane + (r + 1) * SUB, :] = rows.astype(jnp.float32)


def splat_columns(src, dst, tokens):
    flipped = src[...].T
    for n in range(src.shape[0]):
        dst[pl.ds(n * tokens, tokens), :] = jnp.broadcast_to(flipped[:, n : n + 1], (tokens, LANE))


def splat(ref, row):
    return jnp.broadcast_to(ref[pl.ds(row, 1), :], (SUB, LANE))


def steps(total, unroll, body, carry):
    def several(group, carry):
        for k in range(unroll):
            carry = body(group * unroll + k, carry)
        return carry

    return lax.fori_loop(0, total // unroll, several, carry)


def sigmoid(value):
    return 1.0 / (1.0 + jnp.exp(-value))


def conv_at(xs, ws, cb, m, t, taps, parts):
    plane = xs.shape[0] // parts
    conv = cb
    for k in range(taps):
        conv = conv + ws[k] * xs[tile(m * plane + (t + k) * SUB), :]
    return conv


GROUP = 2


def rows_at(refs, t, parts, plane):
    return [[ref[tile(m * plane + t * SUB), :] for m in range(parts)] for ref in refs]


def rates_at(nrates, first, group, parts):
    return [
        nrates[tile(((first + n) * parts + m) * SUB), :] for n in range(group) for m in range(parts)
    ]


def local_body(
    tokens, blocks, nstate, taps,
    x_hbm, draw_hbm, z_hbm, go_hbm, rim_ref, b_ref, c_ref, w_ref, cb_ref, dtb_ref, rate_ref,
    rate_mine_ref,
    pay_ref, skip_ref, dts, dus, gys, us, zfs, sls, sds, xs, bs, cs, nrates,
    ws, raw, sems,
):
    lead = taps - 1
    parts = blocks // SUB
    plane = tokens * SUB
    width = pay_ref.shape[0] // blocks
    copies = [
        pltpu.make_async_copy(src, raw.at[i], sems.at[i])
        for i, src in enumerate((draw_hbm, z_hbm, go_hbm, x_hbm))
    ]
    for copy in copies:
        copy.start()
    spread_rows(w_ref, ws)
    spread_rows(rate_ref, nrates, -LOG2E)
    splat_columns(b_ref, bs, tokens)
    splat_columns(c_ref, cs, tokens)
    place_rim(rim_ref, xs, lead, parts)
    for i, (dst, ahead) in enumerate(((dts, 0), (zfs, 0), (gys, 0), (xs, lead))):
        copies[i].wait()
        spread_tokens(raw.at[i], dst, ahead)
    zero = jnp.zeros((SUB, LANE), jnp.float32)

    for m in range(parts):
        taps_here = [ws[(k * parts + m) * SUB : (k * parts + m + 1) * SUB, :] for k in range(taps)]
        cb = cb_ref[m * SUB : (m + 1) * SUB, :]
        dtb = dtb_ref[m * SUB : (m + 1) * SUB, :]

        def pre(t, totals, m=m, taps_here=taps_here, cb=cb, dtb=dtb):
            here = tile(m * plane + t * SUB)
            conv = conv_at(xs, taps_here, cb, m, t, taps, parts)
            sig_c = sigmoid(conv)
            inner = conv * sig_c
            grow = jnp.exp(dts[here, :] + dtb)
            delta = jnp.log1p(grow)
            zf = zfs[here, :]
            sig_z = sigmoid(zf)
            gof = gys[here, :] * sig_z
            gy = gof * zf
            gys[here, :] = gy
            dts[here, :] = delta
            us[here, :] = inner
            dus[here, :] = delta * inner
            zfs[here, :] = gof * (1.0 + zf * (1.0 - sig_z))
            sls[here, :] = sig_c * (1.0 + conv * (1.0 - sig_c))
            sds[here, :] = grow / (1.0 + grow)
            return totals[0] + delta, totals[1] + gy * inner

        total, skipped = steps(tokens, 8, pre, (zero, zero))
        pay_ref[pl.ds(m * SUB * width + 2 * nstate, SUB, stride=width), :] = total
        skip_ref[m * SUB : (m + 1) * SUB, :] = skipped

    one = jnp.ones((SUB, LANE), jnp.float32)

    def some(group, carry):
        first = group * GROUP
        rates = rates_at(nrates, first, GROUP, parts)

        def scan(t, carry):
            state, cum, pulled = (list(part) for part in carry)
            delta, driven, gy = rows_at((dts, dus, gys), t, parts, plane)
            for n in range(GROUP):
                bb = splat(bs, (first + n) * tokens + t)
                cc = splat(cs, (first + n) * tokens + t)
                for m in range(parts):
                    at = n * parts + m
                    decay = jnp.exp2(delta[m] * rates[at])
                    state[at] = decay * state[at] + driven[m] * bb
                    cum[at] = cum[at] * decay
                    pulled[at] = pulled[at] + cum[at] * (gy[m] * cc)
            return tuple(state), tuple(cum), tuple(pulled)

        count = GROUP * parts
        state, _, pulled = steps(
            tokens, 32, scan, ((zero,) * count, (one,) * count, (zero,) * count)
        )
        for n in range(GROUP):
            for m in range(parts):
                at = n * parts + m
                base = m * SUB * width + first + n
                pay_ref[pl.ds(base, SUB, stride=width), :] = state[at]
                pay_ref[pl.ds(base + nstate, SUB, stride=width), :] = pulled[at]
        return carry

    lax.fori_loop(0, nstate // GROUP, some, 0)


def carry_body(count, mine, span, nstate, width, got_ref, rate_ref, out_ref):
    for blk in range(mine):
        rate = rate_ref[:, blk * span : (blk + 1) * span]
        state = jnp.zeros((nstate, span), jnp.float32)
        back = jnp.zeros((nstate, span), jnp.float32)
        for step in range(count):
            base, outs = (step * mine + blk) * width, (step * mine + blk) * 2 * nstate
            out_ref[outs : outs + nstate, :] = state
            keep = jnp.exp(-rate * got_ref[base + 2 * nstate : base + 2 * nstate + 1, :])
            state = keep * state + got_ref[base : base + nstate, :]
            run = count - 1 - step
            base, outs = (run * mine + blk) * width, (run * mine + blk) * 2 * nstate
            out_ref[outs + nstate : outs + 2 * nstate, :] = back
            keep = jnp.exp(-rate * got_ref[base + 2 * nstate : base + 2 * nstate + 1, :])
            back = keep * back + got_ref[base + nstate : base + 2 * nstate, :]


def fold(sums, out, base, count):
    def some(piece, carry):
        rows = sums[pl.ds(piece * 64 * SUB, 64, stride=SUB), :]
        for s in range(1, SUB):
            rows = rows + sums[pl.ds(piece * 64 * SUB + s, 64, stride=SUB), :]
        out[pl.ds(pl.multiple_of(base + piece * 64, 64), 64), :] = rows
        return carry

    lax.fori_loop(0, count // 64, some, 0)


def grads_body(
    tokens, blocks, nstate, taps,
    in_ref, w_ref, skip_ref, skipped_ref, dts, dus, gys, us, zfs, sls, sds, xs, bs, cs, nrates,
    gx_ref, gz_ref, gd_ref, gb_ref, gc_ref, owed_ref, par_ref,
    ys, gbs, dds, hs, pcs, pbs, ws,
):
    lead = taps - 1
    parts = blocks // SUB
    plane = tokens * SUB
    count = in_ref.shape[0] // blocks
    width = par_ref.shape[0] // blocks
    zero = jnp.zeros((SUB, LANE), jnp.float32)
    spread_rows(w_ref, ws)

    def clear(t, carry):
        for m in range(parts):
            for ref in (ys, gbs, dds):
                ref[tile(m * plane + t * SUB), :] = zero
        return carry

    steps(tokens, 8, clear, 0)
    cells = GROUP * parts

    def some(group, carry):
        first = group * GROUP
        rates = [
            nrates[tile(((first + n) * parts + m) * SUB), :]
            for n in range(GROUP) for m in range(parts)
        ]

        def carried(offset):
            return tuple(
                in_ref[pl.ds(m * SUB * count + offset + first + n, SUB, stride=count), :]
                for n in range(GROUP) for m in range(parts)
            )

        state = carried(0)
        for at in range(cells):
            hs[at * SUB : (at + 1) * SUB, :] = state[at]

        def forward(t, state):
            state = list(state)
            delta, driven, gy, y = (
                [ref[tile(m * plane + t * SUB), :] for m in range(parts)]
                for ref in (dts, dus, gys, ys)
            )
            for n in range(GROUP):
                bb = splat(bs, (first + n) * tokens + t)
                cc = splat(cs, (first + n) * tokens + t)
                pulled = None
                for m in range(parts):
                    at = n * parts + m
                    decay = jnp.exp2(delta[m] * rates[at])
                    now = decay * state[at] + driven[m] * bb
                    state[at] = now
                    hs[tile(((t + 1) * cells + at) * SUB), :] = now
                    y[m] = y[m] + cc * now
                    term = gy[m] * now
                    pulled = term if pulled is None else pulled + term
                pcs[tile((n * tokens + t) * SUB), :] = pulled
            for m in range(parts):
                ys[tile(m * plane + t * SUB), :] = y[m]
            return tuple(state)

        steps(tokens, 32, forward, state)

        def backward(step, carry):
            t = tokens - 1 - step
            back, acc = (list(part) for part in carry)
            delta, driven, gy, gsum, dsum = (
                [ref[tile(m * plane + t * SUB), :] for m in range(parts)]
                for ref in (dts, dus, gys, gbs, dds)
            )
            for n in range(GROUP):
                bb = splat(bs, (first + n) * tokens + t)
                cc = splat(cs, (first + n) * tokens + t)
                pulled = None
                for m in range(parts):
                    at = n * parts + m
                    scaled = delta[m] * rates[at]
                    adj = gy[m] * cc + back[at]
                    gsum[m] = gsum[m] + adj * bb
                    back[at] = jnp.exp2(scaled) * adj
                    both = back[at] * hs[tile((t * cells + at) * SUB), :] * scaled
                    dsum[m] = dsum[m] + both
                    acc[at] = acc[at] + both
                    term = adj * driven[m]
                    pulled = term if pulled is None else pulled + term
                pbs[tile((n * tokens + t) * SUB), :] = pulled
            for m in range(parts):
                gbs[tile(m * plane + t * SUB), :] = gsum[m]
                dds[tile(m * plane + t * SUB), :] = dsum[m]
            return tuple(back), tuple(acc)

        _, acc = steps(tokens, 32, backward, (carried(nstate), (zero,) * cells))
        for n in range(GROUP):
            for m in range(parts):
                base = m * SUB * width + first + n
                par_ref[pl.ds(base, SUB, stride=width), :] = acc[n * parts + m] / -rates[n * parts + m]

        fold(pcs, gc_ref, first * tokens, GROUP * tokens)
        fold(pbs, gb_ref, first * tokens, GROUP * tokens)
        return carry

    lax.fori_loop(0, nstate // GROUP, some, 0)

    for m in range(parts):
        taps_here = [ws[(k * parts + m) * SUB : (k * parts + m + 1) * SUB, :] for k in range(taps)]
        skip = skip_ref[m * SUB : (m + 1) * SUB, :]
        xplane = xs.shape[0] // parts

        def post(t, carry, m=m, skip=skip):
            bias, convb, convw = carry
            here = tile(m * plane + t * SUB)
            gsum, inner = gbs[here, :], us[here, :]
            dd = (gsum * inner + dds[here, :] * (1.0 / LOG2E) / dts[here, :]) * sds[here, :]
            dcv = (gsum * dts[here, :] + gys[here, :] * skip) * sls[here, :]
            dds[here, :] = dd
            gbs[here, :] = dcv
            hs[here, :] = zfs[here, :] * (ys[here, :] + skip * inner)
            convw = tuple(
                convw[k] + dcv * xs[tile(m * xplane + (t + k) * SUB), :] for k in range(taps)
            )
            return bias + dd, convb + dcv, convw

        bias, convb, convw = steps(tokens, 8, post, (zero, zero, (zero,) * taps))
        values = list(convw) + [convb, skipped_ref[m * SUB : (m + 1) * SUB, :], bias]
        for row, value in enumerate(values):
            par_ref[pl.ds(m * SUB * width + nstate + row, SUB, stride=width), :] = value

        def spill(t, carry, m=m, taps_here=taps_here):
            value = None
            for k in range(taps):
                term = taps_here[k] * gbs[tile(m * plane + (t + lead - k) * SUB), :]
                value = term if value is None else value + term
            ys[tile(m * plane + t * SUB), :] = value
            return carry

        whole_steps = (tokens - lead) // 8 * 8
        steps(whole_steps, 8, spill, 0)
        for t in range(whole_steps, tokens - lead):
            spill(t, 0)

        def partial(s):
            value = zero
            for k in range(taps):
                if 0 <= s + lead - k < tokens:
                    value = value + taps_here[k] * gbs[tile(m * plane + (s + lead - k) * SUB), :]
            return value

        for i in range(lead):
            value = partial(tokens - lead + i)
            ys[tile(m * plane + (tokens - lead + i) * SUB), :] = value
            owed_ref[lead + i, m * SUB : (m + 1) * SUB, :] = value
            owed_ref[i, m * SUB : (m + 1) * SUB, :] = partial(i - lead)

    gather_tokens(ys, gx_ref)
    gather_tokens(hs.at[pl.ds(0, parts * plane), :], gz_ref)
    gather_tokens(dds, gd_ref)


def slices(rows, runs):
    blocks, width, lanes = rows.shape
    if blocks % runs == 0:
        return rows.reshape(runs, blocks // runs * width, lanes)
    narrow = blocks * lanes // runs
    return rows.transpose(1, 0, 2).reshape(width, runs, narrow).transpose(1, 0, 2)


def unslices(pieces, blocks, width):
    runs = pieces.shape[0]
    if blocks % runs == 0:
        return pieces.reshape(blocks, width, LANE)
    return pieces.transpose(1, 0, 2).reshape(width, blocks, LANE).transpose(1, 0, 2)


def swap(pieces):
    return lax.all_to_all(pieces, "seq", 0, 0, tiled=True)


def shards(xin, zgate, delta_raw, bmat, cmat, conv_w, conv_b, decay_rate, dskip, dt_bias, grad_out):
    tokens, channels = xin.shape
    nstate, taps = bmat.shape[0], conv_w.shape[0]
    lead = taps - 1
    blocks = channels // LANE
    runs = lax.axis_size("seq")
    me = lax.axis_index("seq")
    mine = max(1, blocks // runs)
    span = channels // runs // mine
    full, edge = tokens * blocks, (tokens + lead) * blocks
    splats, rated = nstate * tokens, nstate * blocks
    vec = lambda rows: pltpu.VMEM((rows, LANE), jnp.float32)
    f32 = lambda *shape: jax.ShapeDtypeStruct(shape, jnp.float32)
    bf16 = lambda *shape: jax.ShapeDtypeStruct(shape, jnp.bfloat16)
    far = lambda *refs: (pltpu.with_memory_space_constraint(ref, pltpu.HBM) for ref in refs)
    limit = lambda mb: pltpu.CompilerParams(vmem_limit_bytes=mb * 1024 * 1024)
    vmem, hbm = (pl.BlockSpec(memory_space=space) for space in (pltpu.VMEM, pltpu.HBM))
    work = nstate * tokens * channels

    def cost(ops, moved):
        return pl.CostEstimate(flops=ops * work, bytes_accessed=moved, transcendentals=work)

    rim = lax.ppermute(
        xin[tokens - lead :].reshape(lead, blocks, LANE), "seq",
        [(i, i + 1) for i in range(runs - 1)],
    )
    cb, dtb, skip = (v.reshape(blocks, LANE) for v in (conv_b, dt_bias, dskip))
    rate_mine = lax.dynamic_slice(decay_rate, (0, me * mine * span), (nstate, mine * span))
    wide = 2 * nstate + 4
    shapes = [full] * 7 + [edge, splats, splats, rated]
    pay, skipped, *factors = pl.pallas_call(
        functools.partial(local_body, tokens, blocks, nstate, taps),
        out_shape=[f32(blocks * wide, LANE), f32(blocks, LANE)] + [vec(r) for r in shapes],
        in_specs=[hbm] * 4 + [vmem] * 7 + [hbm],
        out_specs=[vmem] * 13,
        scratch_shapes=[
            vec(taps * blocks), pltpu.VMEM((4, tokens, channels), jnp.bfloat16),
            pltpu.SemaphoreType.DMA((4,)),
        ],
        compiler_params=limit(LOCAL_MB),
        cost_estimate=cost(9, full * LANE * 36),
        name="local_scan",
    )(
        *far(xin, delta_raw, zgate, grad_out), rim,
        *far(bmat, cmat, conv_w, cb, dtb, decay_rate), rate_mine,
    )
    got = swap(slices(pay.reshape(blocks, wide, LANE), runs))
    carries = pl.pallas_call(
        functools.partial(carry_body, runs, mine, span, nstate, wide),
        out_shape=f32(runs * mine * 2 * nstate, span),
        in_specs=[vmem] * 2,
        out_specs=vmem,
        compiler_params=limit(CARRY_MB),
        name="carry_scan",
    )(got.reshape(runs * mine * wide, span), rate_mine)
    ins = unslices(swap(carries.reshape(runs, mine * 2 * nstate, span)), blocks, 2 * nstate)
    rows = nstate + taps + 3
    rows = rows + (-rows) % SUB
    gx, gz, gd, gb, gc, owed, par = pl.pallas_call(
        functools.partial(grads_body, tokens, blocks, nstate, taps),
        out_shape=(
            bf16(tokens, channels), bf16(tokens, channels), bf16(tokens, channels),
            pltpu.HBM((splats, LANE), jnp.float32), pltpu.HBM((splats, LANE), jnp.float32),
            f32(2 * lead, blocks, LANE), f32(blocks * rows, LANE),
        ),
        in_specs=[vmem] * 15,
        out_specs=tuple([vmem] * 7),
        scratch_shapes=[
            vec(full), vec(full), vec(full), vec((tokens + 1) * GROUP * blocks),
            vec(GROUP * tokens * SUB), vec(GROUP * tokens * SUB), vec(taps * blocks),
        ],
        compiler_params=limit(GRADS_MB),
        cost_estimate=cost(22, nstate * full * LANE),
        name="grads",
    )(ins.reshape(blocks * 2 * nstate, LANE), *far(conv_w, skip), skipped, *factors)
    gb, gc = (jnp.sum(v.reshape(nstate, tokens, LANE), axis=2) for v in (gb, gc))
    returned = lax.ppermute(owed[:lead], "seq", [(i + 1, i) for i in range(runs - 1)])
    last = (owed[lead:] + returned).reshape(lead, channels).astype(jnp.bfloat16)
    gx = lax.dynamic_update_slice(gx, last, (tokens - lead, 0))
    sums = jnp.sum(swap(slices(par.reshape(blocks, rows, LANE), runs)), axis=0)
    every = unslices(swap(jnp.broadcast_to(sums[None], (runs,) + sums.shape)), blocks, rows)
    flat = lambda a, b: every[:, a:b].transpose(1, 0, 2).reshape(b - a, channels)
    line = lambda a: every[:, a].reshape(channels)
    return (
        gx, gz, gd, gb, gc,
        flat(nstate, nstate + taps), line(nstate + taps), flat(0, nstate),
        line(nstate + taps + 1), line(nstate + taps + 2),
    )


def solution(mesh):
    both = P(("dp", "seq"), None)
    across = P(None, ("dp", "seq"))
    return jax.shard_map(
        shards,
        mesh=mesh,
        in_specs=(both, both, both, across, across, P(), P(), P(), P(), P(), both),
        out_specs=(
            both, both, both, across, across,
            P("dp", None), P("dp"), P("dp", None), P("dp"), P("dp"),
        ),
        check_vma=False,
    )
```

```python
import functools
import math

import jax
import jax.numpy as jnp
from jax import lax
from jax.experimental import pallas as pl
from jax.experimental.pallas import tpu as pltpu
from jax.sharding import PartitionSpec as P

LANE = 128
SUB = 8
LOG2E = math.log2(math.e)
LOCAL_MB, CARRY_MB, GRADS_MB = 20, 2, 30


def tile(start):
    return pl.ds(pl.multiple_of(start, SUB), SUB)


def spread_rows(src, dst, scale=None):
    rows, channels = src.shape
    blocks = channels // LANE
    for blk in range(blocks):
        piece = src[:, blk * LANE : (blk + 1) * LANE]
        dst[pl.ds(blk, rows, stride=blocks), :] = piece if scale is None else piece * scale


def spread_tokens(src, dst, lead=0):
    tokens, channels = src.shape
    blocks = channels // LANE
    plane = dst.shape[0] // (blocks // SUB)

    def some(group, carry):
        first = pl.multiple_of(group * 16, 16)
        for blk in range(blocks):
            piece = src[pl.ds(first, 16), blk * LANE : (blk + 1) * LANE].astype(jnp.float32)
            start = blk // SUB * plane + blk % SUB + (first + lead) * SUB
            dst[pl.ds(start, 16, stride=SUB), :] = piece
        return carry

    lax.fori_loop(0, tokens // 16, some, 0)


def gather_tokens(pairs):
    def some(group, carry):
        first = pl.multiple_of(group * 16, 16)
        for src, dst in pairs:
            blocks = dst.shape[1] // LANE
            plane = src.shape[0] // (blocks // SUB)
            for blk in range(blocks):
                start = blk // SUB * plane + blk % SUB + first * SUB
                piece = src[pl.ds(start, 16, stride=SUB), :]
                dst[pl.ds(first, 16), blk * LANE : (blk + 1) * LANE] = piece.astype(dst.dtype)
        return carry

    lax.fori_loop(0, pairs[0][1].shape[0] // 16, some, 0)


def place_rim(rim_ref, xs, lead, parts):
    plane = xs.shape[0] // parts
    for r in range(lead):
        for m in range(parts):
            rows = rim_ref[r, m * SUB : (m + 1) * SUB, :]
            xs[m * plane + r * SUB : m * plane + (r + 1) * SUB, :] = rows.astype(jnp.float32)


def splat_columns(src, dst, tokens):
    flipped = src[...].T
    for n in range(src.shape[0]):
        dst[pl.ds(n * tokens, tokens), :] = jnp.broadcast_to(flipped[:, n : n + 1], (tokens, LANE))


def splat(ref, row):
    return jnp.broadcast_to(ref[pl.ds(row, 1), :], (SUB, LANE))


def steps(total, unroll, body, carry):
    def several(group, carry):
        for k in range(unroll):
            carry = body(group * unroll + k, carry)
        return carry

    return lax.fori_loop(0, total // unroll, several, carry)


def sigmoid(value):
    return 1.0 / (1.0 + jnp.exp(-value))


def conv_at(xs, ws, cb, m, t, taps, parts):
    plane = xs.shape[0] // parts
    conv = cb
    for k in range(taps):
        conv = conv + ws[k] * xs[tile(m * plane + (t + k) * SUB), :]
    return conv


GROUP = 2


def rows_at(refs, t, parts, plane):
    return [[ref[tile(m * plane + t * SUB), :] for m in range(parts)] for ref in refs]


def rates_at(nrates, first, group, parts):
    return [
        nrates[tile(((first + n) * parts + m) * SUB), :] for n in range(group) for m in range(parts)
    ]


def prepare_body(
    tokens, blocks, nstate, taps,
    x_hbm, draw_hbm, z_hbm, go_hbm, b_ref, c_ref, dtb_ref, rate_ref, rate_mine_ref,
    dts, gys, zfs, sds, xs, bs, cs, nrates,
    raw, sems,
):
    parts = blocks // SUB
    plane = tokens * SUB
    copies = [
        pltpu.make_async_copy(src, raw.at[i], sems.at[i])
        for i, src in enumerate((draw_hbm, z_hbm, go_hbm, x_hbm))
    ]
    for copy in copies:
        copy.start()
    spread_rows(rate_ref, nrates, -LOG2E)
    splat_columns(b_ref, bs, tokens)
    splat_columns(c_ref, cs, tokens)
    for i, (dst, ahead) in enumerate(((dts, 0), (zfs, 0), (gys, 0), (xs, taps - 1))):
        copies[i].wait()
        spread_tokens(raw.at[i], dst, ahead)

    for m in range(parts):
        dtb = dtb_ref[m * SUB : (m + 1) * SUB, :]

        def pre(t, carry, m=m, dtb=dtb):
            here = tile(m * plane + t * SUB)
            grow = jnp.exp(dts[here, :] + dtb)
            zf = zfs[here, :]
            sig_z = sigmoid(zf)
            gof = gys[here, :] * sig_z
            dts[here, :] = jnp.log1p(grow)
            sds[here, :] = grow / (1.0 + grow)
            gys[here, :] = gof * zf
            zfs[here, :] = gof * (1.0 + zf * (1.0 - sig_z))
            return carry

        steps(tokens, 16, pre, 0)


def local_body(
    tokens, blocks, nstate, taps,
    rim_ref, w_ref, cb_ref, dts, gys, bs, cs, nrates, xs_in,
    pay_ref, skip_ref, dus, us, sls, xs,
    ws,
):
    lead = taps - 1
    parts = blocks // SUB
    plane = tokens * SUB
    width = pay_ref.shape[0] // blocks
    spread_rows(w_ref, ws)
    place_rim(rim_ref, xs, lead, parts)
    zero = jnp.zeros((SUB, LANE), jnp.float32)

    for m in range(parts):
        taps_here = [ws[(k * parts + m) * SUB : (k * parts + m + 1) * SUB, :] for k in range(taps)]
        cb = cb_ref[m * SUB : (m + 1) * SUB, :]

        def pre(t, totals, m=m, taps_here=taps_here, cb=cb):
            here = tile(m * plane + t * SUB)
            conv = conv_at(xs, taps_here, cb, m, t, taps, parts)
            sig_c = sigmoid(conv)
            inner = conv * sig_c
            delta = dts[here, :]
            us[here, :] = inner
            dus[here, :] = delta * inner
            sls[here, :] = sig_c * (1.0 + conv * (1.0 - sig_c))
            return totals[0] + delta, totals[1] + gys[here, :] * inner

        total, skipped = steps(tokens, 16, pre, (zero, zero))
        pay_ref[pl.ds(m * SUB * width + 2 * nstate, SUB, stride=width), :] = total
        skip_ref[m * SUB : (m + 1) * SUB, :] = skipped

    one = jnp.ones((SUB, LANE), jnp.float32)

    def some(group, carry):
        first = group * GROUP
        rates = rates_at(nrates, first, GROUP, parts)

        def scan(t, carry):
            state, cum, pulled = (list(part) for part in carry)
            delta, driven, gy = rows_at((dts, dus, gys), t, parts, plane)
            for n in range(GROUP):
                bb = splat(bs, (first + n) * tokens + t)
                cc = splat(cs, (first + n) * tokens + t)
                for m in range(parts):
                    at = n * parts + m
                    decay = jnp.exp2(delta[m] * rates[at])
                    state[at] = decay * state[at] + driven[m] * bb
                    cum[at] = cum[at] * decay
                    pulled[at] = pulled[at] + cum[at] * (gy[m] * cc)
            return tuple(state), tuple(cum), tuple(pulled)

        count = GROUP * parts
        state, _, pulled = steps(
            tokens, 64, scan, ((zero,) * count, (one,) * count, (zero,) * count)
        )
        for n in range(GROUP):
            for m in range(parts):
                at = n * parts + m
                base = m * SUB * width + first + n
                pay_ref[pl.ds(base, SUB, stride=width), :] = state[at]
                pay_ref[pl.ds(base + nstate, SUB, stride=width), :] = pulled[at]
        return carry

    lax.fori_loop(0, nstate // GROUP, some, 0)


def carry_body(count, mine, span, nstate, width, got_ref, rate_ref, out_ref):
    for blk in range(mine):
        rate = rate_ref[:, blk * span : (blk + 1) * span]
        state = jnp.zeros((nstate, span), jnp.float32)
        back = jnp.zeros((nstate, span), jnp.float32)
        for step in range(count):
            base, outs = (step * mine + blk) * width, (step * mine + blk) * 2 * nstate
            out_ref[outs : outs + nstate, :] = state
            keep = jnp.exp(-rate * got_ref[base + 2 * nstate : base + 2 * nstate + 1, :])
            state = keep * state + got_ref[base : base + nstate, :]
            run = count - 1 - step
            base, outs = (run * mine + blk) * width, (run * mine + blk) * 2 * nstate
            out_ref[outs + nstate : outs + 2 * nstate, :] = back
            keep = jnp.exp(-rate * got_ref[base + 2 * nstate : base + 2 * nstate + 1, :])
            back = keep * back + got_ref[base + nstate : base + 2 * nstate, :]


def fold(sums, out, base, count):
    def some(piece, carry):
        rows = sums[pl.ds(piece * 64 * SUB, 64, stride=SUB), :]
        for s in range(1, SUB):
            rows = rows + sums[pl.ds(piece * 64 * SUB + s, 64, stride=SUB), :]
        out[pl.ds(pl.multiple_of(base + piece * 64, 64), 64), :] = rows
        return carry

    lax.fori_loop(0, count // 64, some, 0)


def finish_body(blocks, nstate, taps, every_ref, convw_ref, rate_ref, *line_refs):
    rows = every_ref.shape[0] // blocks
    for blk in range(blocks):
        here = slice(blk * LANE, (blk + 1) * LANE)
        rate_ref[:, here] = every_ref[blk * rows : blk * rows + nstate, :]
        convw_ref[:, here] = every_ref[blk * rows + nstate : blk * rows + nstate + taps, :]
    for i, line_ref in enumerate(line_refs):
        line_ref[...] = every_ref[pl.ds(nstate + taps + i, blocks, stride=rows), :]


def grads_body(
    tokens, blocks, nstate, taps,
    in_ref, w_ref, skip_ref, skipped_ref, dts, dus, gys, us, zfs, sls, sds, xs, bs, cs, nrates,
    gx_ref, gz_ref, gd_ref, gb_ref, gc_ref, owed_ref, par_ref,
    ys, gbs, dds, hs, pcs, ws,
):
    lead = taps - 1
    parts = blocks // SUB
    plane = tokens * SUB
    count = in_ref.shape[0] // blocks
    width = par_ref.shape[0] // blocks
    zero = jnp.zeros((SUB, LANE), jnp.float32)
    spread_rows(w_ref, ws)

    def clear(t, carry):
        for m in range(parts):
            for ref in (ys, gbs, dds):
                ref[tile(m * plane + t * SUB), :] = zero
        return carry

    steps(tokens, 8, clear, 0)
    cells = GROUP * parts

    def some(group, carry):
        first = group * GROUP
        rates = [
            nrates[tile(((first + n) * parts + m) * SUB), :]
            for n in range(GROUP) for m in range(parts)
        ]

        def carried(offset):
            return tuple(
                in_ref[pl.ds(m * SUB * count + offset + first + n, SUB, stride=count), :]
                for n in range(GROUP) for m in range(parts)
            )

        state = carried(0)
        for at in range(cells):
            hs[at * SUB : (at + 1) * SUB, :] = state[at]

        def forward(t, state):
            state = list(state)
            delta, driven, gy, y = (
                [ref[tile(m * plane + t * SUB), :] for m in range(parts)]
                for ref in (dts, dus, gys, ys)
            )
            for n in range(GROUP):
                bb = splat(bs, (first + n) * tokens + t)
                cc = splat(cs, (first + n) * tokens + t)
                pulled = None
                for m in range(parts):
                    at = n * parts + m
                    decay = jnp.exp2(delta[m] * rates[at])
                    now = decay * state[at] + driven[m] * bb
                    state[at] = now
                    hs[tile(((t + 1) * cells + at) * SUB), :] = now
                    y[m] = y[m] + cc * now
                    term = gy[m] * now
                    pulled = term if pulled is None else pulled + term
                pcs[tile((n * tokens + t) * SUB), :] = pulled
            for m in range(parts):
                ys[tile(m * plane + t * SUB), :] = y[m]
            return tuple(state)

        steps(tokens, 64, forward, state)
        fold(pcs, gc_ref, first * tokens, GROUP * tokens)

        def backward(step, carry):
            t = tokens - 1 - step
            back, acc = (list(part) for part in carry)
            delta, driven, gy, gsum, dsum = (
                [ref[tile(m * plane + t * SUB), :] for m in range(parts)]
                for ref in (dts, dus, gys, gbs, dds)
            )
            for n in range(GROUP):
                bb = splat(bs, (first + n) * tokens + t)
                cc = splat(cs, (first + n) * tokens + t)
                pulled = None
                for m in range(parts):
                    at = n * parts + m
                    scaled = delta[m] * rates[at]
                    adj = gy[m] * cc + back[at]
                    gsum[m] = gsum[m] + adj * bb
                    back[at] = jnp.exp2(scaled) * adj
                    both = back[at] * hs[tile((t * cells + at) * SUB), :] * scaled
                    dsum[m] = dsum[m] + both
                    acc[at] = acc[at] + both
                    term = adj * driven[m]
                    pulled = term if pulled is None else pulled + term
                gb_ref[pl.ds((first + n) * tokens + t, 1), :] = jnp.sum(pulled, axis=0, keepdims=True)
            for m in range(parts):
                gbs[tile(m * plane + t * SUB), :] = gsum[m]
                dds[tile(m * plane + t * SUB), :] = dsum[m]
            return tuple(back), tuple(acc)

        _, acc = steps(tokens, 64, backward, (carried(nstate), (zero,) * cells))
        for n in range(GROUP):
            for m in range(parts):
                base = m * SUB * width + first + n
                par_ref[pl.ds(base, SUB, stride=width), :] = acc[n * parts + m] / -rates[n * parts + m]

        return carry

    lax.fori_loop(0, nstate // GROUP, some, 0)

    for m in range(parts):
        taps_here = [ws[(k * parts + m) * SUB : (k * parts + m + 1) * SUB, :] for k in range(taps)]
        skip = skip_ref[m * SUB : (m + 1) * SUB, :]
        xplane = xs.shape[0] // parts

        def post(t, carry, m=m, skip=skip):
            bias, convb, convw = carry
            here = tile(m * plane + t * SUB)
            gsum, inner = gbs[here, :], us[here, :]
            dd = (gsum * inner + dds[here, :] * (1.0 / LOG2E) / dts[here, :]) * sds[here, :]
            dcv = (gsum * dts[here, :] + gys[here, :] * skip) * sls[here, :]
            dds[here, :] = dd
            gbs[here, :] = dcv
            hs[here, :] = zfs[here, :] * (ys[here, :] + skip * inner)
            convw = tuple(
                convw[k] + dcv * xs[tile(m * xplane + (t + k) * SUB), :] for k in range(taps)
            )
            return bias + dd, convb + dcv, convw

        bias, convb, convw = steps(tokens, 16, post, (zero, zero, (zero,) * taps))
        values = list(convw) + [convb, skipped_ref[m * SUB : (m + 1) * SUB, :], bias]
        for row, value in enumerate(values):
            par_ref[pl.ds(m * SUB * width + nstate + row, SUB, stride=width), :] = value

        def spill(t, carry, m=m, taps_here=taps_here):
            value = None
            for k in range(taps):
                term = taps_here[k] * gbs[tile(m * plane + (t + lead - k) * SUB), :]
                value = term if value is None else value + term
            ys[tile(m * plane + t * SUB), :] = value
            return carry

        whole_steps = (tokens - lead) // 8 * 8
        steps(whole_steps, 8, spill, 0)
        for t in range(whole_steps, tokens - lead):
            spill(t, 0)

        def partial(s):
            value = zero
            for k in range(taps):
                if 0 <= s + lead - k < tokens:
                    value = value + taps_here[k] * gbs[tile(m * plane + (s + lead - k) * SUB), :]
            return value

        for i in range(lead):
            value = partial(tokens - lead + i)
            ys[tile(m * plane + (tokens - lead + i) * SUB), :] = value
            owed_ref[lead + i, m * SUB : (m + 1) * SUB, :] = value
            owed_ref[i, m * SUB : (m + 1) * SUB, :] = partial(i - lead)

    gather_tokens(((ys, gx_ref), (hs.at[pl.ds(0, parts * plane), :], gz_ref), (dds, gd_ref)))


def slices(rows, runs):
    blocks, width, lanes = rows.shape
    if blocks % runs == 0:
        return rows.reshape(runs, blocks // runs * width, lanes)
    narrow = blocks * lanes // runs
    return rows.transpose(1, 0, 2).reshape(width, runs, narrow).transpose(1, 0, 2)


def unslices(pieces, blocks, width):
    runs = pieces.shape[0]
    if blocks % runs == 0:
        return pieces.reshape(blocks, width, LANE)
    return pieces.transpose(1, 0, 2).reshape(width, blocks, LANE).transpose(1, 0, 2)


def swap(pieces):
    return lax.all_to_all(pieces, "seq", 0, 0, tiled=True)


def shards(xin, zgate, delta_raw, bmat, cmat, conv_w, conv_b, decay_rate, dskip, dt_bias, grad_out):
    tokens, channels = xin.shape
    nstate, taps = bmat.shape[0], conv_w.shape[0]
    lead = taps - 1
    blocks = channels // LANE
    runs = lax.axis_size("seq")
    me = lax.axis_index("seq")
    mine = max(1, blocks // runs)
    span = channels // runs // mine
    full, edge = tokens * blocks, (tokens + lead) * blocks
    splats, rated = nstate * tokens, nstate * blocks
    vec = lambda rows: pltpu.VMEM((rows, LANE), jnp.float32)
    f32 = lambda *shape: jax.ShapeDtypeStruct(shape, jnp.float32)
    bf16 = lambda *shape: jax.ShapeDtypeStruct(shape, jnp.bfloat16)
    far = lambda *refs: (pltpu.with_memory_space_constraint(ref, pltpu.HBM) for ref in refs)
    limit = lambda mb: pltpu.CompilerParams(vmem_limit_bytes=mb * 1024 * 1024)
    vmem, hbm = (pl.BlockSpec(memory_space=space) for space in (pltpu.VMEM, pltpu.HBM))
    work = nstate * tokens * channels

    def cost(ops, moved):
        return pl.CostEstimate(flops=ops * work, bytes_accessed=moved, transcendentals=work)

    rim = lax.ppermute(
        xin[tokens - lead :].reshape(lead, blocks, LANE), "seq",
        [(i, i + 1) for i in range(runs - 1)],
    )
    cb, dtb, skip = (v.reshape(blocks, LANE) for v in (conv_b, dt_bias, dskip))
    rate_mine = lax.dynamic_slice(decay_rate, (0, me * mine * span), (nstate, mine * span))
    wide = 2 * nstate + 4
    dts, gys, zfs, sds, xs, bs, cs, nrates = pl.pallas_call(
        functools.partial(prepare_body, tokens, blocks, nstate, taps),
        out_shape=[vec(r) for r in [full] * 4 + [edge, splats, splats, rated]],
        in_specs=[hbm] * 4 + [vmem] * 4 + [hbm],
        out_specs=[vmem] * 8,
        scratch_shapes=[
            pltpu.VMEM((4, tokens, channels), jnp.bfloat16), pltpu.SemaphoreType.DMA((4,)),
        ],
        compiler_params=limit(LOCAL_MB),
        cost_estimate=cost(3, full * LANE * 8),
        name="prepare",
    )(
        *far(xin, delta_raw, zgate, grad_out, bmat, cmat, dtb, decay_rate), rate_mine
    )
    pay, skipped, dus, us, sls, xs = pl.pallas_call(
        functools.partial(local_body, tokens, blocks, nstate, taps),
        out_shape=[f32(blocks * wide, LANE), f32(blocks, LANE)]
        + [vec(r) for r in [full] * 3 + [edge]],
        in_specs=[vmem] * 9,
        out_specs=[vmem] * 6,
        scratch_shapes=[vec(taps * blocks)],
        input_output_aliases={8: 5},
        compiler_params=limit(LOCAL_MB),
        cost_estimate=cost(9, full * LANE * 36),
        name="local_scan",
    )(rim, *far(conv_w, cb), dts, gys, bs, cs, nrates, xs)
    factors = (dts, dus, gys, us, zfs, sls, sds, xs, bs, cs, nrates)
    got = swap(slices(pay.reshape(blocks, wide, LANE), runs))
    carries = pl.pallas_call(
        functools.partial(carry_body, runs, mine, span, nstate, wide),
        out_shape=f32(runs * mine * 2 * nstate, span),
        in_specs=[vmem] * 2,
        out_specs=vmem,
        compiler_params=limit(CARRY_MB),
        name="carry_scan",
    )(got.reshape(runs * mine * wide, span), rate_mine)
    ins = unslices(swap(carries.reshape(runs, mine * 2 * nstate, span)), blocks, 2 * nstate)
    rows = nstate + taps + 3
    rows = rows + (-rows) % SUB
    gx, gz, gd, gb, gc, owed, par = pl.pallas_call(
        functools.partial(grads_body, tokens, blocks, nstate, taps),
        out_shape=(
            bf16(tokens, channels), bf16(tokens, channels), bf16(tokens, channels),
            pltpu.HBM((splats, LANE), jnp.float32), pltpu.HBM((splats, LANE), jnp.float32),
            f32(2 * lead, blocks, LANE), f32(blocks * rows, LANE),
        ),
        in_specs=[vmem] * 15,
        out_specs=tuple([vmem] * 7),
        scratch_shapes=[
            vec(full), vec(full), vec(full), vec((tokens + 1) * GROUP * blocks),
            vec(GROUP * tokens * SUB),
            vec(taps * blocks),
        ],
        compiler_params=limit(GRADS_MB),
        cost_estimate=cost(22, nstate * full * LANE),
        name="grads",
    )(ins.reshape(blocks * 2 * nstate, LANE), *far(conv_w, skip), skipped, *factors)
    gb, gc = (jnp.sum(v.reshape(nstate, tokens, LANE), axis=2) for v in (gb, gc))
    returned = lax.ppermute(owed[:lead], "seq", [(i + 1, i) for i in range(runs - 1)])
    last = (owed[lead:] + returned).reshape(lead, channels).astype(jnp.bfloat16)
    gx = lax.dynamic_update_slice(gx, last, (tokens - lead, 0))
    sums = jnp.sum(swap(slices(par.reshape(blocks, rows, LANE), runs)), axis=0)
    every = unslices(swap(jnp.broadcast_to(sums[None], (runs,) + sums.shape)), blocks, rows)
    convw, rate, *lines = pl.pallas_call(
        functools.partial(finish_body, blocks, nstate, taps),
        out_shape=[f32(taps, channels), f32(nstate, channels)] + [f32(blocks, LANE)] * 3,
        in_specs=[vmem],
        out_specs=[vmem] * 5,
        compiler_params=limit(CARRY_MB),
        name="finish",
    )(every.reshape(blocks * rows, LANE))
    convb, skips, bias = (v.reshape(channels) for v in lines)
    return gx, gz, gd, gb, gc, convw, convb, rate, skips, bias


def solution(mesh):
    both = P(("dp", "seq"), None)
    across = P(None, ("dp", "seq"))
    return jax.shard_map(
        shards,
        mesh=mesh,
        in_specs=(both, both, both, across, across, P(), P(), P(), P(), P(), both),
        out_specs=(
            both, both, both, across, across,
            P("dp", None), P("dp"), P("dp", None), P("dp"), P("dp"),
        ),
        check_vma=False,
    )
```

```python
import functools
import math

import jax
import jax.numpy as jnp
from jax import lax
from jax.experimental import pallas as pl
from jax.experimental.pallas import tpu as pltpu
from jax.sharding import PartitionSpec as P

LANE = 128
SUB = 8
LOG2E = math.log2(math.e)
LOCAL_MB, CARRY_MB, GRADS_MB = 20, 2, 36


def tile(start):
    return pl.ds(pl.multiple_of(start, SUB), SUB)


def spread_rows(src, dst, scale=None):
    rows, channels = src.shape
    blocks = channels // LANE
    for blk in range(blocks):
        piece = src[:, blk * LANE : (blk + 1) * LANE]
        dst[pl.ds(blk, rows, stride=blocks), :] = piece if scale is None else piece * scale


def spread_tokens(src, dst, lead=0):
    tokens, channels = src.shape
    blocks = channels // LANE
    plane = dst.shape[0] // (blocks // SUB)

    def some(group, carry):
        first = pl.multiple_of(group * 16, 16)
        for blk in range(blocks):
            piece = src[pl.ds(first, 16), blk * LANE : (blk + 1) * LANE].astype(jnp.float32)
            start = blk // SUB * plane + blk % SUB + (first + lead) * SUB
            dst[pl.ds(start, 16, stride=SUB), :] = piece
        return carry

    lax.fori_loop(0, tokens // 16, some, 0)


def gather_tokens(pairs):
    def some(group, carry):
        first = pl.multiple_of(group * 16, 16)
        for src, dst in pairs:
            blocks = dst.shape[1] // LANE
            plane = src.shape[0] // (blocks // SUB)
            for blk in range(blocks):
                start = blk // SUB * plane + blk % SUB + first * SUB
                piece = src[pl.ds(start, 16, stride=SUB), :]
                dst[pl.ds(first, 16), blk * LANE : (blk + 1) * LANE] = piece.astype(dst.dtype)
        return carry

    lax.fori_loop(0, pairs[0][1].shape[0] // 16, some, 0)


def place_rim(rim_ref, xs, lead, parts):
    plane = xs.shape[0] // parts
    for r in range(lead):
        for m in range(parts):
            rows = rim_ref[r, m * SUB : (m + 1) * SUB, :]
            xs[m * plane + r * SUB : m * plane + (r + 1) * SUB, :] = rows.astype(jnp.float32)


def splat_columns(src, dst, tokens):
    flipped = src[...].T
    for n in range(src.shape[0]):
        dst[pl.ds(n * tokens, tokens), :] = jnp.broadcast_to(flipped[:, n : n + 1], (tokens, LANE))


def splat(ref, row):
    return jnp.broadcast_to(ref[pl.ds(row, 1), :], (SUB, LANE))


def steps(total, unroll, body, carry):
    def several(group, carry):
        for k in range(unroll):
            carry = body(group * unroll + k, carry)
        return carry

    return lax.fori_loop(0, total // unroll, several, carry)


def sigmoid(value):
    return 1.0 / (1.0 + jnp.exp(-value))


def conv_at(xs, ws, cb, m, t, taps, parts):
    plane = xs.shape[0] // parts
    conv = cb
    for k in range(taps):
        conv = conv + ws[k] * xs[tile(m * plane + (t + k) * SUB), :]
    return conv


GROUP = 2


def rows_at(refs, t, parts, plane):
    return [[ref[tile(m * plane + t * SUB), :] for m in range(parts)] for ref in refs]


def rates_at(nrates, first, group, parts):
    return [
        nrates[tile(((first + n) * parts + m) * SUB), :] for n in range(group) for m in range(parts)
    ]


def prepare_body(
    tokens, blocks, nstate, taps,
    x_hbm, draw_hbm, z_hbm, go_hbm, b_ref, c_ref, dtb_ref, rate_ref, rate_mine_ref,
    dts, gys, zfs, sds, xs, bs, cs, nrates,
    raw, sems,
):
    parts = blocks // SUB
    plane = tokens * SUB
    copies = [
        pltpu.make_async_copy(src, raw.at[i], sems.at[i])
        for i, src in enumerate((draw_hbm, z_hbm, go_hbm, x_hbm))
    ]
    for copy in copies:
        copy.start()
    spread_rows(rate_ref, nrates, -LOG2E)
    splat_columns(b_ref, bs, tokens)
    splat_columns(c_ref, cs, tokens)
    for i, (dst, ahead) in enumerate(((dts, 0), (zfs, 0), (gys, 0), (xs, taps - 1))):
        copies[i].wait()
        spread_tokens(raw.at[i], dst, ahead)

    for m in range(parts):
        dtb = dtb_ref[m * SUB : (m + 1) * SUB, :]

        def pre(t, carry, m=m, dtb=dtb):
            here = tile(m * plane + t * SUB)
            grow = jnp.exp(dts[here, :] + dtb)
            zf = zfs[here, :]
            sig_z = sigmoid(zf)
            gof = gys[here, :] * sig_z
            dts[here, :] = jnp.log1p(grow)
            sds[here, :] = grow / (1.0 + grow)
            gys[here, :] = gof * zf
            zfs[here, :] = gof * (1.0 + zf * (1.0 - sig_z))
            return carry

        steps(tokens, 16, pre, 0)


def local_body(
    tokens, blocks, nstate, taps,
    rim_ref, w_ref, cb_ref, dts, gys, bs, cs, nrates, xs_in,
    pay_ref, skip_ref, dus, us, sls, xs,
    ws,
):
    lead = taps - 1
    parts = blocks // SUB
    plane = tokens * SUB
    width = pay_ref.shape[0] // blocks
    spread_rows(w_ref, ws)
    place_rim(rim_ref, xs, lead, parts)
    zero = jnp.zeros((SUB, LANE), jnp.float32)

    for m in range(parts):
        taps_here = [ws[(k * parts + m) * SUB : (k * parts + m + 1) * SUB, :] for k in range(taps)]
        cb = cb_ref[m * SUB : (m + 1) * SUB, :]

        def pre(t, totals, m=m, taps_here=taps_here, cb=cb):
            here = tile(m * plane + t * SUB)
            conv = conv_at(xs, taps_here, cb, m, t, taps, parts)
            sig_c = sigmoid(conv)
            inner = conv * sig_c
            delta = dts[here, :]
            us[here, :] = inner
            dus[here, :] = delta * inner
            sls[here, :] = sig_c * (1.0 + conv * (1.0 - sig_c))
            return totals[0] + delta, totals[1] + gys[here, :] * inner

        total, skipped = steps(tokens, 16, pre, (zero, zero))
        pay_ref[pl.ds(m * SUB * width + 2 * nstate, SUB, stride=width), :] = total
        skip_ref[m * SUB : (m + 1) * SUB, :] = skipped

    one = jnp.ones((SUB, LANE), jnp.float32)

    def some(group, carry):
        first = group * GROUP
        rates = rates_at(nrates, first, GROUP, parts)

        def scan(t, carry):
            state, cum, pulled = (list(part) for part in carry)
            delta, driven, gy = rows_at((dts, dus, gys), t, parts, plane)
            for n in range(GROUP):
                bb = splat(bs, (first + n) * tokens + t)
                cc = splat(cs, (first + n) * tokens + t)
                for m in range(parts):
                    at = n * parts + m
                    decay = jnp.exp2(delta[m] * rates[at])
                    state[at] = decay * state[at] + driven[m] * bb
                    cum[at] = cum[at] * decay
                    pulled[at] = pulled[at] + cum[at] * (gy[m] * cc)
            return tuple(state), tuple(cum), tuple(pulled)

        count = GROUP * parts
        state, _, pulled = steps(
            tokens, 64, scan, ((zero,) * count, (one,) * count, (zero,) * count)
        )
        for n in range(GROUP):
            for m in range(parts):
                at = n * parts + m
                base = m * SUB * width + first + n
                pay_ref[pl.ds(base, SUB, stride=width), :] = state[at]
                pay_ref[pl.ds(base + nstate, SUB, stride=width), :] = pulled[at]
        return carry

    lax.fori_loop(0, nstate // GROUP, some, 0)


def carry_body(count, mine, span, nstate, width, got_ref, rate_ref, out_ref):
    for blk in range(mine):
        rate = rate_ref[:, blk * span : (blk + 1) * span]
        state = jnp.zeros((nstate, span), jnp.float32)
        back = jnp.zeros((nstate, span), jnp.float32)
        for step in range(count):
            base, outs = (step * mine + blk) * width, (step * mine + blk) * 2 * nstate
            out_ref[outs : outs + nstate, :] = state
            keep = jnp.exp(-rate * got_ref[base + 2 * nstate : base + 2 * nstate + 1, :])
            state = keep * state + got_ref[base : base + nstate, :]
            run = count - 1 - step
            base, outs = (run * mine + blk) * width, (run * mine + blk) * 2 * nstate
            out_ref[outs + nstate : outs + 2 * nstate, :] = back
            keep = jnp.exp(-rate * got_ref[base + 2 * nstate : base + 2 * nstate + 1, :])
            back = keep * back + got_ref[base + nstate : base + 2 * nstate, :]


def fold(sums, out, base, count):
    def some(piece, carry):
        rows = sums[pl.ds(piece * 64 * SUB, 64, stride=SUB), :]
        for s in range(1, SUB):
            rows = rows + sums[pl.ds(piece * 64 * SUB + s, 64, stride=SUB), :]
        out[pl.ds(pl.multiple_of(base + piece * 64, 64), 64), :] = rows
        return carry

    lax.fori_loop(0, count // 64, some, 0)


def finish_body(blocks, nstate, taps, every_ref, convw_ref, rate_ref, *line_refs):
    rows = every_ref.shape[0] // blocks
    for blk in range(blocks):
        here = slice(blk * LANE, (blk + 1) * LANE)
        rate_ref[:, here] = every_ref[blk * rows : blk * rows + nstate, :]
        convw_ref[:, here] = every_ref[blk * rows + nstate : blk * rows + nstate + taps, :]
    for i, line_ref in enumerate(line_refs):
        line_ref[...] = every_ref[pl.ds(nstate + taps + i, blocks, stride=rows), :]


def grads_body(
    tokens, blocks, nstate, taps,
    in_ref, skip_ref, skipped_ref, dts, dus, gys, us, zfs, sls, sds, xs, bs, cs, nrates,
    dcv_hbm, gz_hbm, dd_hbm, gb_hbm, gc_ref, par_ref,
    ys, gbs, dds, hs, pcs, pbs, sems, sum_sems,
):
    lead = taps - 1
    parts = blocks // SUB
    plane = tokens * SUB
    count = in_ref.shape[0] // blocks
    width = par_ref.shape[0] // blocks
    zero = jnp.zeros((SUB, LANE), jnp.float32)

    def clear(t, carry):
        for m in range(parts):
            for ref in (ys, gbs, dds):
                ref[tile(m * plane + t * SUB), :] = zero
        return carry

    steps(tokens, 8, clear, 0)
    cells = GROUP * parts
    share = GROUP * tokens * SUB

    def leave(group):
        here = pl.ds(pl.multiple_of(group * share, SUB), share)
        return pltpu.make_async_copy(pbs.at[here, :], gb_hbm.at[here, :], sum_sems.at[group])

    def some(group, carry):
        first = group * GROUP
        rates = [
            nrates[tile(((first + n) * parts + m) * SUB), :]
            for n in range(GROUP) for m in range(parts)
        ]

        def carried(offset):
            return tuple(
                in_ref[pl.ds(m * SUB * count + offset + first + n, SUB, stride=count), :]
                for n in range(GROUP) for m in range(parts)
            )

        state = carried(0)
        for at in range(cells):
            hs[at * SUB : (at + 1) * SUB, :] = state[at]

        def forward(t, state):
            state = list(state)
            delta, driven, gy, y = (
                [ref[tile(m * plane + t * SUB), :] for m in range(parts)]
                for ref in (dts, dus, gys, ys)
            )
            for n in range(GROUP):
                bb = splat(bs, (first + n) * tokens + t)
                cc = splat(cs, (first + n) * tokens + t)
                pulled = None
                for m in range(parts):
                    at = n * parts + m
                    decay = jnp.exp2(delta[m] * rates[at])
                    now = decay * state[at] + driven[m] * bb
                    state[at] = now
                    hs[tile(((t + 1) * cells + at) * SUB), :] = now
                    y[m] = y[m] + cc * now
                    term = gy[m] * now
                    pulled = term if pulled is None else pulled + term
                pcs[tile((n * tokens + t) * SUB), :] = pulled
            for m in range(parts):
                ys[tile(m * plane + t * SUB), :] = y[m]
            return tuple(state)

        steps(tokens, 64, forward, state)
        fold(pcs, gc_ref, first * tokens, GROUP * tokens)

        def backward(step, carry):
            t = tokens - 1 - step
            back, acc = (list(part) for part in carry)
            delta, driven, gy, gsum, dsum = (
                [ref[tile(m * plane + t * SUB), :] for m in range(parts)]
                for ref in (dts, dus, gys, gbs, dds)
            )
            for n in range(GROUP):
                bb = splat(bs, (first + n) * tokens + t)
                cc = splat(cs, (first + n) * tokens + t)
                pulled = None
                for m in range(parts):
                    at = n * parts + m
                    scaled = delta[m] * rates[at]
                    adj = gy[m] * cc + back[at]
                    gsum[m] = gsum[m] + adj * bb
                    back[at] = jnp.exp2(scaled) * adj
                    both = back[at] * hs[tile((t * cells + at) * SUB), :] * scaled
                    dsum[m] = dsum[m] + both
                    acc[at] = acc[at] + both
                    term = adj * driven[m]
                    pulled = term if pulled is None else pulled + term
                pbs[tile(((first + n) * tokens + t) * SUB), :] = pulled
            for m in range(parts):
                gbs[tile(m * plane + t * SUB), :] = gsum[m]
                dds[tile(m * plane + t * SUB), :] = dsum[m]
            return tuple(back), tuple(acc)

        _, acc = steps(tokens, 64, backward, (carried(nstate), (zero,) * cells))
        for n in range(GROUP):
            for m in range(parts):
                base = m * SUB * width + first + n
                par_ref[pl.ds(base, SUB, stride=width), :] = acc[n * parts + m] / -rates[n * parts + m]

        leave(group).start()
        return carry

    lax.fori_loop(0, nstate // GROUP, some, 0)

    copies = []
    for m in range(parts):
        skip = skip_ref[m * SUB : (m + 1) * SUB, :]
        xplane = xs.shape[0] // parts

        def post(t, carry, m=m, skip=skip):
            bias, convb, convw = carry
            here = tile(m * plane + t * SUB)
            gsum, inner = gbs[here, :], us[here, :]
            dd = (gsum * inner + dds[here, :] * (1.0 / LOG2E) / dts[here, :]) * sds[here, :]
            dcv = (gsum * dts[here, :] + gys[here, :] * skip) * sls[here, :]
            dds[here, :] = dd
            gbs[here, :] = dcv
            hs[here, :] = zfs[here, :] * (ys[here, :] + skip * inner)
            convw = tuple(
                convw[k] + dcv * xs[tile(m * xplane + (t + k) * SUB), :] for k in range(taps)
            )
            return bias + dd, convb + dcv, convw

        bias, convb, convw = steps(tokens, 16, post, (zero, zero, (zero,) * taps))
        values = list(convw) + [convb, skipped_ref[m * SUB : (m + 1) * SUB, :], bias]
        for row, value in enumerate(values):
            par_ref[pl.ds(m * SUB * width + nstate + row, SUB, stride=width), :] = value

        here = pl.ds(m * plane, plane)
        for i, (src, dst) in enumerate(((gbs, dcv_hbm), (hs, gz_hbm), (dds, dd_hbm))):
            copies.append(pltpu.make_async_copy(src.at[here, :], dst.at[here, :], sems.at[m, i]))
            copies[-1].start()

    for copy in copies:
        copy.wait()
    for group in range(nstate // GROUP):
        leave(group).wait()


def outs_body(
    tokens, blocks, taps,
    w_ref, dcv_hbm, gz_hbm, dd_hbm,
    gx_ref, gz_ref, gd_ref, owed_ref,
    gbs, gzs, dds, ys, ws, sems,
):
    lead = taps - 1
    parts = blocks // SUB
    plane = tokens * SUB
    zero = jnp.zeros((SUB, LANE), jnp.float32)
    copies = [
        pltpu.make_async_copy(src, dst, sems.at[i])
        for i, (src, dst) in enumerate(((dcv_hbm, gbs), (gz_hbm, gzs), (dd_hbm, dds)))
    ]
    for copy in copies:
        copy.start()
    spread_rows(w_ref, ws)
    copies[0].wait()
    for m in range(parts):
        taps_here = [ws[(k * parts + m) * SUB : (k * parts + m + 1) * SUB, :] for k in range(taps)]

        def spill(t, carry, m=m, taps_here=taps_here):
            value = None
            for k in range(taps):
                term = taps_here[k] * gbs[tile(m * plane + (t + lead - k) * SUB), :]
                value = term if value is None else value + term
            ys[tile(m * plane + t * SUB), :] = value
            return carry

        whole_steps = (tokens - lead) // 8 * 8
        steps(whole_steps, 8, spill, 0)
        for t in range(whole_steps, tokens - lead):
            spill(t, 0)

        def partial(s):
            value = zero
            for k in range(taps):
                if 0 <= s + lead - k < tokens:
                    value = value + taps_here[k] * gbs[tile(m * plane + (s + lead - k) * SUB), :]
            return value

        for i in range(lead):
            value = partial(tokens - lead + i)
            ys[tile(m * plane + (tokens - lead + i) * SUB), :] = value
            owed_ref[lead + i, m * SUB : (m + 1) * SUB, :] = value
            owed_ref[i, m * SUB : (m + 1) * SUB, :] = partial(i - lead)

    copies[1].wait()
    copies[2].wait()
    gather_tokens(((ys, gx_ref), (gzs, gz_ref), (dds, gd_ref)))


def slices(rows, runs):
    blocks, width, lanes = rows.shape
    if blocks % runs == 0:
        return rows.reshape(runs, blocks // runs * width, lanes)
    narrow = blocks * lanes // runs
    return rows.transpose(1, 0, 2).reshape(width, runs, narrow).transpose(1, 0, 2)


def unslices(pieces, blocks, width):
    runs = pieces.shape[0]
    if blocks % runs == 0:
        return pieces.reshape(blocks, width, LANE)
    return pieces.transpose(1, 0, 2).reshape(width, blocks, LANE).transpose(1, 0, 2)


def swap(pieces):
    return lax.all_to_all(pieces, "seq", 0, 0, tiled=True)


def shards(xin, zgate, delta_raw, bmat, cmat, conv_w, conv_b, decay_rate, dskip, dt_bias, grad_out):
    tokens, channels = xin.shape
    nstate, taps = bmat.shape[0], conv_w.shape[0]
    lead = taps - 1
    blocks = channels // LANE
    runs = lax.axis_size("seq")
    me = lax.axis_index("seq")
    mine = max(1, blocks // runs)
    span = channels // runs // mine
    full, edge = tokens * blocks, (tokens + lead) * blocks
    splats, rated = nstate * tokens, nstate * blocks
    vec = lambda rows: pltpu.VMEM((rows, LANE), jnp.float32)
    f32 = lambda *shape: jax.ShapeDtypeStruct(shape, jnp.float32)
    bf16 = lambda *shape: jax.ShapeDtypeStruct(shape, jnp.bfloat16)
    far = lambda *refs: (pltpu.with_memory_space_constraint(ref, pltpu.HBM) for ref in refs)
    limit = lambda mb: pltpu.CompilerParams(vmem_limit_bytes=mb * 1024 * 1024)
    vmem, hbm = (pl.BlockSpec(memory_space=space) for space in (pltpu.VMEM, pltpu.HBM))
    work = nstate * tokens * channels

    def cost(ops, moved):
        return pl.CostEstimate(flops=ops * work, bytes_accessed=moved, transcendentals=work)

    rim = lax.ppermute(
        xin[tokens - lead :].reshape(lead, blocks, LANE), "seq",
        [(i, i + 1) for i in range(runs - 1)],
    )
    cb, dtb, skip = (v.reshape(blocks, LANE) for v in (conv_b, dt_bias, dskip))
    rate_mine = lax.dynamic_slice(decay_rate, (0, me * mine * span), (nstate, mine * span))
    wide = 2 * nstate + 4
    dts, gys, zfs, sds, xs, bs, cs, nrates = pl.pallas_call(
        functools.partial(prepare_body, tokens, blocks, nstate, taps),
        out_shape=[vec(r) for r in [full] * 4 + [edge, splats, splats, rated]],
        in_specs=[hbm] * 4 + [vmem] * 4 + [hbm],
        out_specs=[vmem] * 8,
        scratch_shapes=[
            pltpu.VMEM((4, tokens, channels), jnp.bfloat16), pltpu.SemaphoreType.DMA((4,)),
        ],
        compiler_params=limit(LOCAL_MB),
        cost_estimate=cost(3, full * LANE * 8),
        name="prepare",
    )(
        *far(xin, delta_raw, zgate, grad_out, bmat, cmat, dtb, decay_rate), rate_mine
    )
    pay, skipped, dus, us, sls, xs = pl.pallas_call(
        functools.partial(local_body, tokens, blocks, nstate, taps),
        out_shape=[f32(blocks * wide, LANE), f32(blocks, LANE)]
        + [vec(r) for r in [full] * 3 + [edge]],
        in_specs=[vmem] * 9,
        out_specs=[vmem] * 6,
        scratch_shapes=[vec(taps * blocks)],
        input_output_aliases={8: 5},
        compiler_params=limit(LOCAL_MB),
        cost_estimate=cost(9, full * LANE * 36),
        name="local_scan",
    )(rim, *far(conv_w, cb), dts, gys, bs, cs, nrates, xs)
    factors = (dts, dus, gys, us, zfs, sls, sds, xs, bs, cs, nrates)
    got = swap(slices(pay.reshape(blocks, wide, LANE), runs))
    carries = pl.pallas_call(
        functools.partial(carry_body, runs, mine, span, nstate, wide),
        out_shape=f32(runs * mine * 2 * nstate, span),
        in_specs=[vmem] * 2,
        out_specs=vmem,
        compiler_params=limit(CARRY_MB),
        name="carry_scan",
    )(got.reshape(runs * mine * wide, span), rate_mine)
    ins = unslices(swap(carries.reshape(runs, mine * 2 * nstate, span)), blocks, 2 * nstate)
    rows = nstate + taps + 3
    rows = rows + (-rows) % SUB
    away = lambda rows: pltpu.HBM((rows, LANE), jnp.float32)
    dcv, gz, dd, gb, gc, par = pl.pallas_call(
        functools.partial(grads_body, tokens, blocks, nstate, taps),
        out_shape=(*[away(full)] * 3, away(splats * SUB), away(splats), f32(blocks * rows, LANE)),
        in_specs=[vmem] * 14,
        out_specs=(*[hbm] * 4, vmem, vmem),
        scratch_shapes=[
            vec(full), vec(full), vec(full), vec((tokens + 1) * GROUP * blocks),
            vec(GROUP * tokens * SUB), vec(splats * SUB), pltpu.SemaphoreType.DMA((blocks // SUB, 3)),
            pltpu.SemaphoreType.DMA((nstate // GROUP,)),
        ],
        compiler_params=limit(GRADS_MB),
        cost_estimate=cost(22, nstate * full * LANE),
        name="grads",
    )(ins.reshape(blocks * 2 * nstate, LANE), *far(skip), skipped, *factors)
    summed = swap(slices(par.reshape(blocks, rows, LANE), runs))
    gx, gz, gd, owed = pl.pallas_call(
        functools.partial(outs_body, tokens, blocks, taps),
        out_shape=(*[pltpu.HBM((tokens, channels), jnp.bfloat16)] * 3, f32(2 * lead, blocks, LANE)),
        in_specs=[vmem] + [hbm] * 3,
        out_specs=tuple([vmem] * 4),
        scratch_shapes=[
            vec(full), vec(full), vec(full), vec(full), vec(taps * blocks),
            pltpu.SemaphoreType.DMA((3,)),
        ],
        compiler_params=limit(GRADS_MB),
        cost_estimate=pl.CostEstimate(
            flops=8 * full * LANE, bytes_accessed=5 * full * LANE * 4, transcendentals=0
        ),
        name="outs",
    )(*far(conv_w, dcv, gz, dd))
    sums = jnp.sum(summed, axis=0)
    gc = jnp.sum(gc.reshape(nstate, tokens, LANE), axis=2)
    sums, owed, gc = lax.optimization_barrier((sums, owed, gc))
    gb = jnp.sum(gb.reshape(nstate, tokens, SUB, LANE), axis=(2, 3))
    returned = lax.ppermute(owed[:lead], "seq", [(i + 1, i) for i in range(runs - 1)])
    last = (owed[lead:] + returned).reshape(lead, channels).astype(jnp.bfloat16)
    gx = lax.dynamic_update_slice(gx, last, (tokens - lead, 0))
    every = unslices(swap(jnp.broadcast_to(sums[None], (runs,) + sums.shape)), blocks, rows)
    convw, rate, *lines = pl.pallas_call(
        functools.partial(finish_body, blocks, nstate, taps),
        out_shape=[f32(taps, channels), f32(nstate, channels)] + [f32(blocks, LANE)] * 3,
        in_specs=[vmem],
        out_specs=[vmem] * 5,
        compiler_params=limit(CARRY_MB),
        name="finish",
    )(every.reshape(blocks * rows, LANE))
    convb, skips, bias = (v.reshape(channels) for v in lines)
    return gx, gz, gd, gb, gc, convw, convb, rate, skips, bias


def solution(mesh):
    both = P(("dp", "seq"), None)
    across = P(None, ("dp", "seq"))
    return jax.shard_map(
        shards,
        mesh=mesh,
        in_specs=(both, both, both, across, across, P(), P(), P(), P(), P(), both),
        out_specs=(
            both, both, both, across, across,
            P("dp", None), P("dp"), P("dp", None), P("dp"), P("dp"),
        ),
        check_vma=False,
    )
```

```python
import functools
import math

import jax
import jax.numpy as jnp
from jax import lax
from jax.experimental import pallas as pl
from jax.experimental.pallas import tpu as pltpu
from jax.sharding import PartitionSpec as P

LANE = 128
SUB = 8
LOG2E = math.log2(math.e)
LOCAL_MB, CARRY_MB, GRADS_MB = 20, 2, 36


def tile(start):
    return pl.ds(pl.multiple_of(start, SUB), SUB)


def spread_rows(src, dst, scale=None):
    rows, channels = src.shape
    blocks = channels // LANE
    for blk in range(blocks):
        piece = src[:, blk * LANE : (blk + 1) * LANE]
        dst[pl.ds(blk, rows, stride=blocks), :] = piece if scale is None else piece * scale


def spread_tokens(src, dst, lead=0):
    tokens, channels = src.shape
    blocks = channels // LANE
    plane = dst.shape[0] // (blocks // SUB)

    def some(group, carry):
        first = pl.multiple_of(group * 16, 16)
        for blk in range(blocks):
            piece = src[pl.ds(first, 16), blk * LANE : (blk + 1) * LANE].astype(jnp.float32)
            start = blk // SUB * plane + blk % SUB + (first + lead) * SUB
            dst[pl.ds(start, 16, stride=SUB), :] = piece
        return carry

    lax.fori_loop(0, tokens // 16, some, 0)


def gather_tokens(pairs):
    def some(group, carry):
        first = pl.multiple_of(group * 16, 16)
        for src, dst in pairs:
            blocks = dst.shape[1] // LANE
            plane = src.shape[0] // (blocks // SUB)
            for blk in range(blocks):
                start = blk // SUB * plane + blk % SUB + first * SUB
                piece = src[pl.ds(start, 16, stride=SUB), :]
                dst[pl.ds(first, 16), blk * LANE : (blk + 1) * LANE] = piece.astype(dst.dtype)
        return carry

    lax.fori_loop(0, pairs[0][1].shape[0] // 16, some, 0)


def place_rim(rim_ref, xs, lead, parts):
    plane = xs.shape[0] // parts
    for r in range(lead):
        for m in range(parts):
            rows = rim_ref[r, m * SUB : (m + 1) * SUB, :]
            xs[m * plane + r * SUB : m * plane + (r + 1) * SUB, :] = rows.astype(jnp.float32)


def splat_columns(src, dst, tokens):
    flipped = src[...].T
    for n in range(src.shape[0]):
        dst[pl.ds(n * tokens, tokens), :] = jnp.broadcast_to(flipped[:, n : n + 1], (tokens, LANE))


def splat(ref, row):
    return jnp.broadcast_to(ref[pl.ds(row, 1), :], (SUB, LANE))


def steps(total, unroll, body, carry):
    def several(group, carry):
        for k in range(unroll):
            carry = body(group * unroll + k, carry)
        return carry

    return lax.fori_loop(0, total // unroll, several, carry)


def sigmoid(value):
    return 1.0 / (1.0 + jnp.exp(-value))


def conv_at(xs, ws, cb, m, t, taps, parts):
    plane = xs.shape[0] // parts
    conv = cb
    for k in range(taps):
        conv = conv + ws[k] * xs[tile(m * plane + (t + k) * SUB), :]
    return conv


GROUP = 2


def rows_at(refs, t, parts, plane):
    return [[ref[tile(m * plane + t * SUB), :] for m in range(parts)] for ref in refs]


def rates_at(nrates, first, group, parts):
    return [
        nrates[tile(((first + n) * parts + m) * SUB), :] for n in range(group) for m in range(parts)
    ]


def prepare_body(
    tokens, blocks, nstate, taps,
    x_hbm, draw_hbm, z_hbm, go_hbm, b_ref, c_ref, dtb_ref, rate_ref, rate_mine_ref,
    dts, gys, zfs, sds, xs, bs, cs, nrates,
    raw, sems,
):
    parts = blocks // SUB
    plane = tokens * SUB
    copies = [
        pltpu.make_async_copy(src, raw.at[i], sems.at[i])
        for i, src in enumerate((draw_hbm, z_hbm, go_hbm, x_hbm))
    ]
    for copy in copies:
        copy.start()
    spread_rows(rate_ref, nrates, -LOG2E)
    splat_columns(b_ref, bs, tokens)
    splat_columns(c_ref, cs, tokens)
    for i, (dst, ahead) in enumerate(((dts, 0), (zfs, 0), (gys, 0), (xs, taps - 1))):
        copies[i].wait()
        spread_tokens(raw.at[i], dst, ahead)

    for m in range(parts):
        dtb = dtb_ref[m * SUB : (m + 1) * SUB, :]

        def pre(t, carry, m=m, dtb=dtb):
            here = tile(m * plane + t * SUB)
            grow = jnp.exp(dts[here, :] + dtb)
            zf = zfs[here, :]
            sig_z = sigmoid(zf)
            gof = gys[here, :] * sig_z
            dts[here, :] = jnp.log1p(grow)
            sds[here, :] = grow / (1.0 + grow)
            gys[here, :] = gof * zf
            zfs[here, :] = gof * (1.0 + zf * (1.0 - sig_z))
            return carry

        steps(tokens, 16, pre, 0)


def local_body(
    tokens, blocks, nstate, taps,
    rim_ref, w_ref, cb_ref, dts, gys, bs, cs, nrates, xs_in,
    pay_ref, skip_ref, dus, us, sls, xs,
    ws,
):
    lead = taps - 1
    parts = blocks // SUB
    plane = tokens * SUB
    width = pay_ref.shape[0] // blocks
    spread_rows(w_ref, ws)
    place_rim(rim_ref, xs, lead, parts)
    zero = jnp.zeros((SUB, LANE), jnp.float32)

    for m in range(parts):
        taps_here = [ws[(k * parts + m) * SUB : (k * parts + m + 1) * SUB, :] for k in range(taps)]
        cb = cb_ref[m * SUB : (m + 1) * SUB, :]

        def pre(t, totals, m=m, taps_here=taps_here, cb=cb):
            here = tile(m * plane + t * SUB)
            conv = conv_at(xs, taps_here, cb, m, t, taps, parts)
            sig_c = sigmoid(conv)
            inner = conv * sig_c
            delta = dts[here, :]
            us[here, :] = inner
            dus[here, :] = delta * inner
            sls[here, :] = sig_c * (1.0 + conv * (1.0 - sig_c))
            return totals[0] + delta, totals[1] + gys[here, :] * inner

        total, skipped = steps(tokens, 16, pre, (zero, zero))
        pay_ref[pl.ds(m * SUB * width + 2 * nstate, SUB, stride=width), :] = total
        skip_ref[m * SUB : (m + 1) * SUB, :] = skipped

    one = jnp.ones((SUB, LANE), jnp.float32)

    def some(group, carry):
        first = group * GROUP
        rates = rates_at(nrates, first, GROUP, parts)

        def scan(t, carry):
            state, cum, pulled = (list(part) for part in carry)
            delta, driven, gy = rows_at((dts, dus, gys), t, parts, plane)
            for n in range(GROUP):
                bb = splat(bs, (first + n) * tokens + t)
                cc = splat(cs, (first + n) * tokens + t)
                for m in range(parts):
                    at = n * parts + m
                    decay = jnp.exp2(delta[m] * rates[at])
                    state[at] = decay * state[at] + driven[m] * bb
                    cum[at] = cum[at] * decay
                    pulled[at] = pulled[at] + cum[at] * (gy[m] * cc)
            return tuple(state), tuple(cum), tuple(pulled)

        count = GROUP * parts
        state, _, pulled = steps(
            tokens, 64, scan, ((zero,) * count, (one,) * count, (zero,) * count)
        )
        for n in range(GROUP):
            for m in range(parts):
                at = n * parts + m
                base = m * SUB * width + first + n
                pay_ref[pl.ds(base, SUB, stride=width), :] = state[at]
                pay_ref[pl.ds(base + nstate, SUB, stride=width), :] = pulled[at]
        return carry

    lax.fori_loop(0, nstate // GROUP, some, 0)


def carry_body(count, mine, span, nstate, width, got_ref, rate_ref, out_ref):
    for blk in range(mine):
        rate = rate_ref[:, blk * span : (blk + 1) * span]
        state = jnp.zeros((nstate, span), jnp.float32)
        back = jnp.zeros((nstate, span), jnp.float32)
        for step in range(count):
            base, outs = (step * mine + blk) * width, (step * mine + blk) * 2 * nstate
            out_ref[outs : outs + nstate, :] = state
            keep = jnp.exp(-rate * got_ref[base + 2 * nstate : base + 2 * nstate + 1, :])
            state = keep * state + got_ref[base : base + nstate, :]
            run = count - 1 - step
            base, outs = (run * mine + blk) * width, (run * mine + blk) * 2 * nstate
            out_ref[outs + nstate : outs + 2 * nstate, :] = back
            keep = jnp.exp(-rate * got_ref[base + 2 * nstate : base + 2 * nstate + 1, :])
            back = keep * back + got_ref[base + nstate : base + 2 * nstate, :]


def fold(sums, out, base, count):
    def some(piece, carry):
        rows = sums[pl.ds(piece * 64 * SUB, 64, stride=SUB), :]
        for s in range(1, SUB):
            rows = rows + sums[pl.ds(piece * 64 * SUB + s, 64, stride=SUB), :]
        out[pl.ds(pl.multiple_of(base + piece * 64, 64), 64), :] = rows
        return carry

    lax.fori_loop(0, count // 64, some, 0)


def finish_body(blocks, nstate, taps, every_ref, convw_ref, rate_ref, *line_refs):
    rows = every_ref.shape[0] // blocks
    for blk in range(blocks):
        here = slice(blk * LANE, (blk + 1) * LANE)
        rate_ref[:, here] = every_ref[blk * rows : blk * rows + nstate, :]
        convw_ref[:, here] = every_ref[blk * rows + nstate : blk * rows + nstate + taps, :]
    for i, line_ref in enumerate(line_refs):
        line_ref[...] = every_ref[pl.ds(nstate + taps + i, blocks, stride=rows), :]


def grads_body(
    tokens, blocks, nstate, taps,
    in_ref, skip_ref, skipped_ref, dts, dus, gys, us, zfs, sls, sds, xs, bs, cs, nrates,
    dcv_hbm, gz_hbm, dd_hbm, gb_hbm, gc_hbm, par_ref,
    ys, gbs, dds, hs, pcs, pbs, sems, sum_sems,
):
    lead = taps - 1
    parts = blocks // SUB
    plane = tokens * SUB
    count = in_ref.shape[0] // blocks
    width = par_ref.shape[0] // blocks
    zero = jnp.zeros((SUB, LANE), jnp.float32)

    def clear(t, carry):
        for m in range(parts):
            for ref in (ys, gbs, dds):
                ref[tile(m * plane + t * SUB), :] = zero
        return carry

    steps(tokens, 8, clear, 0)
    cells = GROUP * parts
    share = GROUP * tokens * SUB

    def leave(group, src, dst, which):
        here = pl.ds(pl.multiple_of(group * share, SUB), share)
        return pltpu.make_async_copy(src.at[here, :], dst.at[here, :], sum_sems.at[which, group])

    def some(group, carry):
        first = group * GROUP
        rates = [
            nrates[tile(((first + n) * parts + m) * SUB), :]
            for n in range(GROUP) for m in range(parts)
        ]

        def carried(offset):
            return tuple(
                in_ref[pl.ds(m * SUB * count + offset + first + n, SUB, stride=count), :]
                for n in range(GROUP) for m in range(parts)
            )

        state = carried(0)
        for at in range(cells):
            hs[at * SUB : (at + 1) * SUB, :] = state[at]

        def forward(t, state):
            state = list(state)
            delta, driven, gy, y = (
                [ref[tile(m * plane + t * SUB), :] for m in range(parts)]
                for ref in (dts, dus, gys, ys)
            )
            for n in range(GROUP):
                bb = splat(bs, (first + n) * tokens + t)
                cc = splat(cs, (first + n) * tokens + t)
                pulled = None
                for m in range(parts):
                    at = n * parts + m
                    decay = jnp.exp2(delta[m] * rates[at])
                    now = decay * state[at] + driven[m] * bb
                    state[at] = now
                    hs[tile(((t + 1) * cells + at) * SUB), :] = now
                    y[m] = y[m] + cc * now
                    term = gy[m] * now
                    pulled = term if pulled is None else pulled + term
                pcs[tile(((first + n) * tokens + t) * SUB), :] = pulled
            for m in range(parts):
                ys[tile(m * plane + t * SUB), :] = y[m]
            return tuple(state)

        steps(tokens, 64, forward, state)
        leave(group, pcs, gc_hbm, 0).start()

        def backward(step, carry):
            t = tokens - 1 - step
            back, acc = (list(part) for part in carry)
            delta, driven, gy, gsum, dsum = (
                [ref[tile(m * plane + t * SUB), :] for m in range(parts)]
                for ref in (dts, dus, gys, gbs, dds)
            )
            for n in range(GROUP):
                bb = splat(bs, (first + n) * tokens + t)
                cc = splat(cs, (first + n) * tokens + t)
                pulled = None
                for m in range(parts):
                    at = n * parts + m
                    scaled = delta[m] * rates[at]
                    adj = gy[m] * cc + back[at]
                    gsum[m] = gsum[m] + adj * bb
                    back[at] = jnp.exp2(scaled) * adj
                    both = back[at] * hs[tile((t * cells + at) * SUB), :] * scaled
                    dsum[m] = dsum[m] + both
                    acc[at] = acc[at] + both
                    term = adj * driven[m]
                    pulled = term if pulled is None else pulled + term
                pbs[tile(((first + n) * tokens + t) * SUB), :] = pulled
            for m in range(parts):
                gbs[tile(m * plane + t * SUB), :] = gsum[m]
                dds[tile(m * plane + t * SUB), :] = dsum[m]
            return tuple(back), tuple(acc)

        _, acc = steps(tokens, 64, backward, (carried(nstate), (zero,) * cells))
        for n in range(GROUP):
            for m in range(parts):
                base = m * SUB * width + first + n
                par_ref[pl.ds(base, SUB, stride=width), :] = acc[n * parts + m] / -rates[n * parts + m]

        leave(group, pbs, gb_hbm, 1).start()
        return carry

    lax.fori_loop(0, nstate // GROUP, some, 0)

    copies = []
    for m in range(parts):
        skip = skip_ref[m * SUB : (m + 1) * SUB, :]
        xplane = xs.shape[0] // parts

        def post(t, carry, m=m, skip=skip):
            bias, convb, convw = carry
            here = tile(m * plane + t * SUB)
            gsum, inner = gbs[here, :], us[here, :]
            dd = (gsum * inner + dds[here, :] * (1.0 / LOG2E) / dts[here, :]) * sds[here, :]
            dcv = (gsum * dts[here, :] + gys[here, :] * skip) * sls[here, :]
            dds[here, :] = dd
            gbs[here, :] = dcv
            hs[here, :] = zfs[here, :] * (ys[here, :] + skip * inner)
            convw = tuple(
                convw[k] + dcv * xs[tile(m * xplane + (t + k) * SUB), :] for k in range(taps)
            )
            return bias + dd, convb + dcv, convw

        bias, convb, convw = steps(tokens, 16, post, (zero, zero, (zero,) * taps))
        values = list(convw) + [convb, skipped_ref[m * SUB : (m + 1) * SUB, :], bias]
        for row, value in enumerate(values):
            par_ref[pl.ds(m * SUB * width + nstate + row, SUB, stride=width), :] = value

        here = pl.ds(m * plane, plane)
        for i, (src, dst) in enumerate(((gbs, dcv_hbm), (hs, gz_hbm), (dds, dd_hbm))):
            copies.append(pltpu.make_async_copy(src.at[here, :], dst.at[here, :], sems.at[m, i]))
            copies[-1].start()

    for copy in copies:
        copy.wait()
    for group in range(nstate // GROUP):
        leave(group, pcs, gc_hbm, 0).wait()
        leave(group, pbs, gb_hbm, 1).wait()


def outs_body(
    tokens, blocks, taps,
    w_ref, dcv_hbm, gz_hbm, dd_hbm, sum_hbm,
    gx_ref, gz_ref, gd_ref, gc_ref, owed_ref,
    gbs, gzs, dds, pcs, ys, ws, sems,
):
    lead = taps - 1
    parts = blocks // SUB
    plane = tokens * SUB
    zero = jnp.zeros((SUB, LANE), jnp.float32)
    copies = [
        pltpu.make_async_copy(src, dst, sems.at[i])
        for i, (src, dst) in enumerate(
            ((dcv_hbm, gbs), (gz_hbm, gzs), (dd_hbm, dds), (sum_hbm, pcs))
        )
    ]
    for copy in copies:
        copy.start()
    spread_rows(w_ref, ws)
    copies[0].wait()
    for m in range(parts):
        taps_here = [ws[(k * parts + m) * SUB : (k * parts + m + 1) * SUB, :] for k in range(taps)]

        def spill(t, carry, m=m, taps_here=taps_here):
            value = None
            for k in range(taps):
                term = taps_here[k] * gbs[tile(m * plane + (t + lead - k) * SUB), :]
                value = term if value is None else value + term
            ys[tile(m * plane + t * SUB), :] = value
            return carry

        whole_steps = (tokens - lead) // 8 * 8
        steps(whole_steps, 8, spill, 0)
        for t in range(whole_steps, tokens - lead):
            spill(t, 0)

        def partial(s):
            value = zero
            for k in range(taps):
                if 0 <= s + lead - k < tokens:
                    value = value + taps_here[k] * gbs[tile(m * plane + (s + lead - k) * SUB), :]
            return value

        for i in range(lead):
            value = partial(tokens - lead + i)
            ys[tile(m * plane + (tokens - lead + i) * SUB), :] = value
            owed_ref[lead + i, m * SUB : (m + 1) * SUB, :] = value
            owed_ref[i, m * SUB : (m + 1) * SUB, :] = partial(i - lead)

    copies[1].wait()
    copies[2].wait()
    gather_tokens(((ys, gx_ref), (gzs, gz_ref), (dds, gd_ref)))
    copies[3].wait()
    fold(pcs, gc_ref, 0, gc_ref.shape[0])


def slices(rows, runs):
    blocks, width, lanes = rows.shape
    if blocks % runs == 0:
        return rows.reshape(runs, blocks // runs * width, lanes)
    narrow = blocks * lanes // runs
    return rows.transpose(1, 0, 2).reshape(width, runs, narrow).transpose(1, 0, 2)


def unslices(pieces, blocks, width):
    runs = pieces.shape[0]
    if blocks % runs == 0:
        return pieces.reshape(blocks, width, LANE)
    return pieces.transpose(1, 0, 2).reshape(width, blocks, LANE).transpose(1, 0, 2)


def swap(pieces):
    return lax.all_to_all(pieces, "seq", 0, 0, tiled=True)


def shards(xin, zgate, delta_raw, bmat, cmat, conv_w, conv_b, decay_rate, dskip, dt_bias, grad_out):
    tokens, channels = xin.shape
    nstate, taps = bmat.shape[0], conv_w.shape[0]
    lead = taps - 1
    blocks = channels // LANE
    runs = lax.axis_size("seq")
    me = lax.axis_index("seq")
    mine = max(1, blocks // runs)
    span = channels // runs // mine
    full, edge = tokens * blocks, (tokens + lead) * blocks
    splats, rated = nstate * tokens, nstate * blocks
    vec = lambda rows: pltpu.VMEM((rows, LANE), jnp.float32)
    f32 = lambda *shape: jax.ShapeDtypeStruct(shape, jnp.float32)
    bf16 = lambda *shape: jax.ShapeDtypeStruct(shape, jnp.bfloat16)
    far = lambda *refs: (pltpu.with_memory_space_constraint(ref, pltpu.HBM) for ref in refs)
    limit = lambda mb: pltpu.CompilerParams(vmem_limit_bytes=mb * 1024 * 1024)
    vmem, hbm = (pl.BlockSpec(memory_space=space) for space in (pltpu.VMEM, pltpu.HBM))
    work = nstate * tokens * channels

    def cost(ops, moved):
        return pl.CostEstimate(flops=ops * work, bytes_accessed=moved, transcendentals=work)

    rim = lax.ppermute(
        xin[tokens - lead :].reshape(lead, blocks, LANE), "seq",
        [(i, i + 1) for i in range(runs - 1)],
    )
    cb, dtb, skip = (v.reshape(blocks, LANE) for v in (conv_b, dt_bias, dskip))
    rate_mine = lax.dynamic_slice(decay_rate, (0, me * mine * span), (nstate, mine * span))
    wide = 2 * nstate + 4
    dts, gys, zfs, sds, xs, bs, cs, nrates = pl.pallas_call(
        functools.partial(prepare_body, tokens, blocks, nstate, taps),
        out_shape=[vec(r) for r in [full] * 4 + [edge, splats, splats, rated]],
        in_specs=[hbm] * 4 + [vmem] * 4 + [hbm],
        out_specs=[vmem] * 8,
        scratch_shapes=[
            pltpu.VMEM((4, tokens, channels), jnp.bfloat16), pltpu.SemaphoreType.DMA((4,)),
        ],
        compiler_params=limit(LOCAL_MB),
        cost_estimate=cost(3, full * LANE * 8),
        name="prepare",
    )(
        *far(xin, delta_raw, zgate, grad_out, bmat, cmat, dtb, decay_rate), rate_mine
    )
    pay, skipped, dus, us, sls, xs = pl.pallas_call(
        functools.partial(local_body, tokens, blocks, nstate, taps),
        out_shape=[f32(blocks * wide, LANE), f32(blocks, LANE)]
        + [vec(r) for r in [full] * 3 + [edge]],
        in_specs=[vmem] * 9,
        out_specs=[vmem] * 6,
        scratch_shapes=[vec(taps * blocks)],
        input_output_aliases={8: 5},
        compiler_params=limit(LOCAL_MB),
        cost_estimate=cost(9, full * LANE * 36),
        name="local_scan",
    )(rim, *far(conv_w, cb), dts, gys, bs, cs, nrates, xs)
    factors = (dts, dus, gys, us, zfs, sls, sds, xs, bs, cs, nrates)
    got = swap(slices(pay.reshape(blocks, wide, LANE), runs))
    carries = pl.pallas_call(
        functools.partial(carry_body, runs, mine, span, nstate, wide),
        out_shape=f32(runs * mine * 2 * nstate, span),
        in_specs=[vmem] * 2,
        out_specs=vmem,
        compiler_params=limit(CARRY_MB),
        name="carry_scan",
    )(got.reshape(runs * mine * wide, span), rate_mine)
    ins = unslices(swap(carries.reshape(runs, mine * 2 * nstate, span)), blocks, 2 * nstate)
    rows = nstate + taps + 3
    rows = rows + (-rows) % SUB
    away = lambda rows: pltpu.HBM((rows, LANE), jnp.float32)
    dcv, gz, dd, gb, gc, par = pl.pallas_call(
        functools.partial(grads_body, tokens, blocks, nstate, taps),
        out_shape=(*[away(full)] * 3, *[away(splats * SUB)] * 2, f32(blocks * rows, LANE)),
        in_specs=[vmem] * 14,
        out_specs=(*[hbm] * 5, vmem),
        scratch_shapes=[
            vec(full), vec(full), vec(full), vec((tokens + 1) * GROUP * blocks),
            vec(splats * SUB), vec(splats * SUB), pltpu.SemaphoreType.DMA((blocks // SUB, 3)),
            pltpu.SemaphoreType.DMA((2, nstate // GROUP)),
        ],
        compiler_params=limit(GRADS_MB),
        cost_estimate=cost(22, nstate * full * LANE),
        name="grads",
    )(ins.reshape(blocks * 2 * nstate, LANE), *far(skip), skipped, *factors)
    summed = swap(slices(par.reshape(blocks, rows, LANE), runs))
    gx, gz, gd, gc, owed = pl.pallas_call(
        functools.partial(outs_body, tokens, blocks, taps),
        out_shape=(
            *[pltpu.HBM((tokens, channels), jnp.bfloat16)] * 3, away(splats),
            f32(2 * lead, blocks, LANE),
        ),
        in_specs=[vmem] + [hbm] * 4,
        out_specs=tuple([vmem] * 5),
        scratch_shapes=[
            vec(full), vec(full), vec(full), vec(splats * SUB), vec(full), vec(taps * blocks),
            pltpu.SemaphoreType.DMA((4,)),
        ],
        compiler_params=limit(GRADS_MB),
        cost_estimate=pl.CostEstimate(
            flops=8 * full * LANE, bytes_accessed=5 * full * LANE * 4, transcendentals=0
        ),
        name="outs",
    )(*far(conv_w, dcv, gz, dd, gc))
    sums = jnp.sum(summed, axis=0)
    sums, owed = lax.optimization_barrier((sums, owed))
    gb = jnp.sum(gb.reshape(nstate, tokens, SUB, LANE), axis=(2, 3))
    gc = jnp.sum(gc.reshape(nstate, tokens, LANE), axis=2)
    returned = lax.ppermute(owed[:lead], "seq", [(i + 1, i) for i in range(runs - 1)])
    last = (owed[lead:] + returned).reshape(lead, channels).astype(jnp.bfloat16)
    gx = lax.dynamic_update_slice(gx, last, (tokens - lead, 0))
    every = unslices(swap(jnp.broadcast_to(sums[None], (runs,) + sums.shape)), blocks, rows)
    convw, rate, *lines = pl.pallas_call(
        functools.partial(finish_body, blocks, nstate, taps),
        out_shape=[f32(taps, channels), f32(nstate, channels)] + [f32(blocks, LANE)] * 3,
        in_specs=[vmem],
        out_specs=[vmem] * 5,
        compiler_params=limit(CARRY_MB),
        name="finish",
    )(every.reshape(blocks * rows, LANE))
    convb, skips, bias = (v.reshape(channels) for v in lines)
    return gx, gz, gd, gb, gc, convw, convb, rate, skips, bias


def solution(mesh):
    both = P(("dp", "seq"), None)
    across = P(None, ("dp", "seq"))
    return jax.shard_map(
        shards,
        mesh=mesh,
        in_specs=(both, both, both, across, across, P(), P(), P(), P(), P(), both),
        out_specs=(
            both, both, both, across, across,
            P("dp", None), P("dp"), P("dp", None), P("dp"), P("dp"),
        ),
        check_vma=False,
    )
```

```python
import functools
import math

import jax
import jax.numpy as jnp
from jax import lax
from jax.experimental import pallas as pl
from jax.experimental.pallas import tpu as pltpu
from jax.sharding import PartitionSpec as P

LANE = 128
SUB = 8
LOG2E = math.log2(math.e)
LOCAL_MB, CARRY_MB, GRADS_MB = 20, 2, 36


def tile(start):
    return pl.ds(pl.multiple_of(start, SUB), SUB)


def spread_rows(src, dst, scale=None):
    rows, channels = src.shape
    blocks = channels // LANE
    for blk in range(blocks):
        piece = src[:, blk * LANE : (blk + 1) * LANE]
        dst[pl.ds(blk, rows, stride=blocks), :] = piece if scale is None else piece * scale


def spread_tokens(src, dst, lead=0):
    tokens, channels = src.shape
    blocks = channels // LANE
    plane = dst.shape[0] // (blocks // SUB)

    def some(group, carry):
        first = pl.multiple_of(group * 16, 16)
        for blk in range(blocks):
            piece = src[pl.ds(first, 16), blk * LANE : (blk + 1) * LANE].astype(jnp.float32)
            start = blk // SUB * plane + blk % SUB + (first + lead) * SUB
            dst[pl.ds(start, 16, stride=SUB), :] = piece
        return carry

    lax.fori_loop(0, tokens // 16, some, 0)


def gather_tokens(pairs):
    def some(group, carry):
        first = pl.multiple_of(group * 16, 16)
        for src, dst in pairs:
            blocks = dst.shape[1] // LANE
            plane = src.shape[0] // (blocks // SUB)
            for blk in range(blocks):
                start = blk // SUB * plane + blk % SUB + first * SUB
                piece = src[pl.ds(start, 16, stride=SUB), :]
                dst[pl.ds(first, 16), blk * LANE : (blk + 1) * LANE] = piece.astype(dst.dtype)
        return carry

    lax.fori_loop(0, pairs[0][1].shape[0] // 16, some, 0)


def place_rim(rim_ref, xs, lead, parts):
    plane = xs.shape[0] // parts
    for r in range(lead):
        for m in range(parts):
            rows = rim_ref[r, m * SUB : (m + 1) * SUB, :]
            xs[m * plane + r * SUB : m * plane + (r + 1) * SUB, :] = rows.astype(jnp.float32)


def splat_columns(src, dst, tokens):
    flipped = src[...].T
    for n in range(src.shape[0]):
        dst[pl.ds(n * tokens, tokens), :] = jnp.broadcast_to(flipped[:, n : n + 1], (tokens, LANE))


def splat(ref, row):
    return jnp.broadcast_to(ref[pl.ds(row, 1), :], (SUB, LANE))


def steps(total, unroll, body, carry):
    def several(group, carry):
        for k in range(unroll):
            carry = body(group * unroll + k, carry)
        return carry

    return lax.fori_loop(0, total // unroll, several, carry)


def sigmoid(value):
    return 1.0 / (1.0 + jnp.exp(-value))


def conv_at(xs, ws, cb, m, t, taps, parts):
    plane = xs.shape[0] // parts
    conv = cb
    for k in range(taps):
        conv = conv + ws[k] * xs[tile(m * plane + (t + k) * SUB), :]
    return conv


GROUP = 2


def rows_at(refs, t, parts, plane):
    return [[ref[tile(m * plane + t * SUB), :] for m in range(parts)] for ref in refs]


def rates_at(nrates, first, group, parts):
    return [
        nrates[tile(((first + n) * parts + m) * SUB), :] for n in range(group) for m in range(parts)
    ]


def prepare_body(
    tokens, blocks, nstate, taps,
    x_hbm, draw_hbm, z_hbm, go_hbm, b_ref, c_ref, dtb_ref, rate_ref, rate_mine_ref,
    dts, gys, zfs, sds, xs, bs, cs, nrates,
    raw, sems,
):
    parts = blocks // SUB
    plane = tokens * SUB
    copies = [
        pltpu.make_async_copy(src, raw.at[i], sems.at[i])
        for i, src in enumerate((draw_hbm, z_hbm, go_hbm, x_hbm))
    ]
    for copy in copies:
        copy.start()
    spread_rows(rate_ref, nrates, -LOG2E)
    splat_columns(b_ref, bs, tokens)
    splat_columns(c_ref, cs, tokens)
    for i, (dst, ahead) in enumerate(((dts, 0), (zfs, 0), (gys, 0), (xs, taps - 1))):
        copies[i].wait()
        spread_tokens(raw.at[i], dst, ahead)

    for m in range(parts):
        dtb = dtb_ref[m * SUB : (m + 1) * SUB, :]

        def pre(t, carry, m=m, dtb=dtb):
            here = tile(m * plane + t * SUB)
            grow = jnp.exp(dts[here, :] + dtb)
            zf = zfs[here, :]
            sig_z = sigmoid(zf)
            gof = gys[here, :] * sig_z
            dts[here, :] = jnp.log1p(grow)
            sds[here, :] = grow / (1.0 + grow)
            gys[here, :] = gof * zf
            zfs[here, :] = gof * (1.0 + zf * (1.0 - sig_z))
            return carry

        steps(tokens, 32, pre, 0)


def local_body(
    tokens, blocks, nstate, taps,
    rim_ref, w_ref, cb_ref, dts, gys, bs, cs, nrates, xs_in,
    pay_ref, skip_ref, dus, us, sls, xs,
    ws,
):
    lead = taps - 1
    parts = blocks // SUB
    plane = tokens * SUB
    width = pay_ref.shape[0] // blocks
    spread_rows(w_ref, ws)
    place_rim(rim_ref, xs, lead, parts)
    zero = jnp.zeros((SUB, LANE), jnp.float32)

    for m in range(parts):
        taps_here = [ws[(k * parts + m) * SUB : (k * parts + m + 1) * SUB, :] for k in range(taps)]
        cb = cb_ref[m * SUB : (m + 1) * SUB, :]

        def pre(t, totals, m=m, taps_here=taps_here, cb=cb):
            here = tile(m * plane + t * SUB)
            conv = conv_at(xs, taps_here, cb, m, t, taps, parts)
            sig_c = sigmoid(conv)
            inner = conv * sig_c
            delta = dts[here, :]
            us[here, :] = inner
            dus[here, :] = delta * inner
            sls[here, :] = sig_c * (1.0 + conv * (1.0 - sig_c))
            return totals[0] + delta, totals[1] + gys[here, :] * inner

        total, skipped = steps(tokens, 32, pre, (zero, zero))
        pay_ref[pl.ds(m * SUB * width + 2 * nstate, SUB, stride=width), :] = total
        skip_ref[m * SUB : (m + 1) * SUB, :] = skipped

    one = jnp.ones((SUB, LANE), jnp.float32)

    def some(group, carry):
        first = group * GROUP
        rates = rates_at(nrates, first, GROUP, parts)

        def scan(t, carry):
            state, cum, pulled = (list(part) for part in carry)
            delta, driven, gy = rows_at((dts, dus, gys), t, parts, plane)
            for n in range(GROUP):
                bb = splat(bs, (first + n) * tokens + t)
                cc = splat(cs, (first + n) * tokens + t)
                for m in range(parts):
                    at = n * parts + m
                    decay = jnp.exp2(delta[m] * rates[at])
                    state[at] = decay * state[at] + driven[m] * bb
                    cum[at] = cum[at] * decay
                    pulled[at] = pulled[at] + cum[at] * (gy[m] * cc)
            return tuple(state), tuple(cum), tuple(pulled)

        count = GROUP * parts
        state, _, pulled = steps(
            tokens, 64, scan, ((zero,) * count, (one,) * count, (zero,) * count)
        )
        for n in range(GROUP):
            for m in range(parts):
                at = n * parts + m
                base = m * SUB * width + first + n
                pay_ref[pl.ds(base, SUB, stride=width), :] = state[at]
                pay_ref[pl.ds(base + nstate, SUB, stride=width), :] = pulled[at]
        return carry

    lax.fori_loop(0, nstate // GROUP, some, 0)


def carry_body(count, mine, span, nstate, width, got_ref, rate_ref, out_ref):
    for blk in range(mine):
        rate = rate_ref[:, blk * span : (blk + 1) * span]
        state = jnp.zeros((nstate, span), jnp.float32)
        back = jnp.zeros((nstate, span), jnp.float32)
        for step in range(count):
            base, outs = (step * mine + blk) * width, (step * mine + blk) * 2 * nstate
            out_ref[outs : outs + nstate, :] = state
            keep = jnp.exp(-rate * got_ref[base + 2 * nstate : base + 2 * nstate + 1, :])
            state = keep * state + got_ref[base : base + nstate, :]
            run = count - 1 - step
            base, outs = (run * mine + blk) * width, (run * mine + blk) * 2 * nstate
            out_ref[outs + nstate : outs + 2 * nstate, :] = back
            keep = jnp.exp(-rate * got_ref[base + 2 * nstate : base + 2 * nstate + 1, :])
            back = keep * back + got_ref[base + nstate : base + 2 * nstate, :]


def fold(sums, out, base, count):
    def some(piece, carry):
        rows = sums[pl.ds(piece * 64 * SUB, 64, stride=SUB), :]
        for s in range(1, SUB):
            rows = rows + sums[pl.ds(piece * 64 * SUB + s, 64, stride=SUB), :]
        out[pl.ds(pl.multiple_of(base + piece * 64, 64), 64), :] = rows
        return carry

    lax.fori_loop(0, count // 64, some, 0)


def finish_body(blocks, nstate, taps, every_ref, convw_ref, rate_ref, *line_refs):
    rows = every_ref.shape[0] // blocks
    for blk in range(blocks):
        here = slice(blk * LANE, (blk + 1) * LANE)
        rate_ref[:, here] = every_ref[blk * rows : blk * rows + nstate, :]
        convw_ref[:, here] = every_ref[blk * rows + nstate : blk * rows + nstate + taps, :]
    for i, line_ref in enumerate(line_refs):
        line_ref[...] = every_ref[pl.ds(nstate + taps + i, blocks, stride=rows), :]


def grads_body(
    tokens, blocks, nstate, taps,
    in_ref, skip_ref, skipped_ref, dts, dus, gys, us, zfs, sls, sds, xs, bs, cs, nrates,
    dcv_hbm, gz_hbm, dd_hbm, gb_hbm, gc_hbm, par_ref,
    ys, gbs, dds, hs, pcs, pbs, sems, sum_sems,
):
    lead = taps - 1
    parts = blocks // SUB
    plane = tokens * SUB
    count = in_ref.shape[0] // blocks
    width = par_ref.shape[0] // blocks
    zero = jnp.zeros((SUB, LANE), jnp.float32)

    def clear(t, carry):
        for m in range(parts):
            for ref in (ys, gbs, dds):
                ref[tile(m * plane + t * SUB), :] = zero
        return carry

    steps(tokens, 8, clear, 0)
    cells = GROUP * parts
    share = GROUP * tokens * SUB

    def leave(group, src, dst, which):
        here = pl.ds(pl.multiple_of(group * share, SUB), share)
        return pltpu.make_async_copy(src.at[here, :], dst.at[here, :], sum_sems.at[which, group])

    def some(group, carry):
        first = group * GROUP
        rates = [
            nrates[tile(((first + n) * parts + m) * SUB), :]
            for n in range(GROUP) for m in range(parts)
        ]

        def carried(offset):
            return tuple(
                in_ref[pl.ds(m * SUB * count + offset + first + n, SUB, stride=count), :]
                for n in range(GROUP) for m in range(parts)
            )

        state = carried(0)
        for at in range(cells):
            hs[at * SUB : (at + 1) * SUB, :] = state[at]

        def forward(t, state):
            state = list(state)
            delta, driven, gy, y = (
                [ref[tile(m * plane + t * SUB), :] for m in range(parts)]
                for ref in (dts, dus, gys, ys)
            )
            for n in range(GROUP):
                bb = splat(bs, (first + n) * tokens + t)
                cc = splat(cs, (first + n) * tokens + t)
                pulled = None
                for m in range(parts):
                    at = n * parts + m
                    decay = jnp.exp2(delta[m] * rates[at])
                    now = decay * state[at] + driven[m] * bb
                    state[at] = now
                    hs[tile(((t + 1) * cells + at) * SUB), :] = now
                    y[m] = y[m] + cc * now
                    term = gy[m] * now
                    pulled = term if pulled is None else pulled + term
                pcs[tile(((first + n) * tokens + t) * SUB), :] = pulled
            for m in range(parts):
                ys[tile(m * plane + t * SUB), :] = y[m]
            return tuple(state)

        steps(tokens, 64, forward, state)
        leave(group, pcs, gc_hbm, 0).start()

        def backward(step, carry):
            t = tokens - 1 - step
            back, acc = (list(part) for part in carry)
            delta, driven, gy, gsum, dsum = (
                [ref[tile(m * plane + t * SUB), :] for m in range(parts)]
                for ref in (dts, dus, gys, gbs, dds)
            )
            for n in range(GROUP):
                bb = splat(bs, (first + n) * tokens + t)
                cc = splat(cs, (first + n) * tokens + t)
                pulled = None
                for m in range(parts):
                    at = n * parts + m
                    scaled = delta[m] * rates[at]
                    adj = gy[m] * cc + back[at]
                    gsum[m] = gsum[m] + adj * bb
                    back[at] = jnp.exp2(scaled) * adj
                    both = back[at] * hs[tile((t * cells + at) * SUB), :] * scaled
                    dsum[m] = dsum[m] + both
                    acc[at] = acc[at] + both
                    term = adj * driven[m]
                    pulled = term if pulled is None else pulled + term
                pbs[tile(((first + n) * tokens + t) * SUB), :] = pulled
            for m in range(parts):
                gbs[tile(m * plane + t * SUB), :] = gsum[m]
                dds[tile(m * plane + t * SUB), :] = dsum[m]
            return tuple(back), tuple(acc)

        _, acc = steps(tokens, 64, backward, (carried(nstate), (zero,) * cells))
        for n in range(GROUP):
            for m in range(parts):
                base = m * SUB * width + first + n
                par_ref[pl.ds(base, SUB, stride=width), :] = acc[n * parts + m] / -rates[n * parts + m]

        leave(group, pbs, gb_hbm, 1).start()
        return carry

    lax.fori_loop(0, nstate // GROUP, some, 0)

    copies = []
    for m in range(parts):
        skip = skip_ref[m * SUB : (m + 1) * SUB, :]
        xplane = xs.shape[0] // parts

        def post(t, carry, m=m, skip=skip):
            bias, convb, convw = carry
            here = tile(m * plane + t * SUB)
            gsum, inner = gbs[here, :], us[here, :]
            dd = (gsum * inner + dds[here, :] * (1.0 / LOG2E) / dts[here, :]) * sds[here, :]
            dcv = (gsum * dts[here, :] + gys[here, :] * skip) * sls[here, :]
            dds[here, :] = dd
            gbs[here, :] = dcv
            hs[here, :] = zfs[here, :] * (ys[here, :] + skip * inner)
            convw = tuple(
                convw[k] + dcv * xs[tile(m * xplane + (t + k) * SUB), :] for k in range(taps)
            )
            return bias + dd, convb + dcv, convw

        bias, convb, convw = steps(tokens, 32, post, (zero, zero, (zero,) * taps))
        values = list(convw) + [convb, skipped_ref[m * SUB : (m + 1) * SUB, :], bias]
        for row, value in enumerate(values):
            par_ref[pl.ds(m * SUB * width + nstate + row, SUB, stride=width), :] = value

        here = pl.ds(m * plane, plane)
        for i, (src, dst) in enumerate(((gbs, dcv_hbm), (hs, gz_hbm), (dds, dd_hbm))):
            copies.append(pltpu.make_async_copy(src.at[here, :], dst.at[here, :], sems.at[m, i]))
            copies[-1].start()

    for copy in copies:
        copy.wait()
    for group in range(nstate // GROUP):
        leave(group, pcs, gc_hbm, 0).wait()
        leave(group, pbs, gb_hbm, 1).wait()


def outs_body(
    tokens, blocks, taps,
    w_ref, dcv_hbm, gz_hbm, dd_hbm, sum_hbm,
    gx_ref, gz_ref, gd_ref, gc_ref, owed_ref,
    gbs, gzs, dds, pcs, ys, ws, sems,
):
    lead = taps - 1
    parts = blocks // SUB
    plane = tokens * SUB
    zero = jnp.zeros((SUB, LANE), jnp.float32)
    copies = [
        pltpu.make_async_copy(src, dst, sems.at[i])
        for i, (src, dst) in enumerate(
            ((dcv_hbm, gbs), (gz_hbm, gzs), (dd_hbm, dds), (sum_hbm, pcs))
        )
    ]
    for copy in copies:
        copy.start()
    spread_rows(w_ref, ws)
    copies[0].wait()
    for m in range(parts):
        taps_here = [ws[(k * parts + m) * SUB : (k * parts + m + 1) * SUB, :] for k in range(taps)]

        def spill(t, carry, m=m, taps_here=taps_here):
            value = None
            for k in range(taps):
                term = taps_here[k] * gbs[tile(m * plane + (t + lead - k) * SUB), :]
                value = term if value is None else value + term
            ys[tile(m * plane + t * SUB), :] = value
            return carry

        whole_steps = (tokens - lead) // 8 * 8
        steps(whole_steps, 8, spill, 0)
        for t in range(whole_steps, tokens - lead):
            spill(t, 0)

        def partial(s):
            value = zero
            for k in range(taps):
                if 0 <= s + lead - k < tokens:
                    value = value + taps_here[k] * gbs[tile(m * plane + (s + lead - k) * SUB), :]
            return value

        for i in range(lead):
            value = partial(tokens - lead + i)
            ys[tile(m * plane + (tokens - lead + i) * SUB), :] = value
            owed_ref[lead + i, m * SUB : (m + 1) * SUB, :] = value
            owed_ref[i, m * SUB : (m + 1) * SUB, :] = partial(i - lead)

    copies[1].wait()
    copies[2].wait()
    gather_tokens(((ys, gx_ref), (gzs, gz_ref), (dds, gd_ref)))
    copies[3].wait()
    fold(pcs, gc_ref, 0, gc_ref.shape[0])


def slices(rows, runs):
    blocks, width, lanes = rows.shape
    if blocks % runs == 0:
        return rows.reshape(runs, blocks // runs * width, lanes)
    narrow = blocks * lanes // runs
    return rows.transpose(1, 0, 2).reshape(width, runs, narrow).transpose(1, 0, 2)


def unslices(pieces, blocks, width):
    runs = pieces.shape[0]
    if blocks % runs == 0:
        return pieces.reshape(blocks, width, LANE)
    return pieces.transpose(1, 0, 2).reshape(width, blocks, LANE).transpose(1, 0, 2)


def swap(pieces):
    return lax.all_to_all(pieces, "seq", 0, 0, tiled=True)


def shards(xin, zgate, delta_raw, bmat, cmat, conv_w, conv_b, decay_rate, dskip, dt_bias, grad_out):
    tokens, channels = xin.shape
    nstate, taps = bmat.shape[0], conv_w.shape[0]
    lead = taps - 1
    blocks = channels // LANE
    runs = lax.axis_size("seq")
    me = lax.axis_index("seq")
    mine = max(1, blocks // runs)
    span = channels // runs // mine
    full, edge = tokens * blocks, (tokens + lead) * blocks
    splats, rated = nstate * tokens, nstate * blocks
    vec = lambda rows: pltpu.VMEM((rows, LANE), jnp.float32)
    f32 = lambda *shape: jax.ShapeDtypeStruct(shape, jnp.float32)
    bf16 = lambda *shape: jax.ShapeDtypeStruct(shape, jnp.bfloat16)
    far = lambda *refs: (pltpu.with_memory_space_constraint(ref, pltpu.HBM) for ref in refs)
    limit = lambda mb: pltpu.CompilerParams(vmem_limit_bytes=mb * 1024 * 1024)
    vmem, hbm = (pl.BlockSpec(memory_space=space) for space in (pltpu.VMEM, pltpu.HBM))
    work = nstate * tokens * channels

    def cost(ops, moved):
        return pl.CostEstimate(flops=ops * work, bytes_accessed=moved, transcendentals=work)

    rim = lax.ppermute(
        xin[tokens - lead :].reshape(lead, blocks, LANE), "seq",
        [(i, i + 1) for i in range(runs - 1)],
    )
    cb, dtb, skip = (v.reshape(blocks, LANE) for v in (conv_b, dt_bias, dskip))
    rate_mine = lax.dynamic_slice(decay_rate, (0, me * mine * span), (nstate, mine * span))
    wide = 2 * nstate + 4
    dts, gys, zfs, sds, xs, bs, cs, nrates = pl.pallas_call(
        functools.partial(prepare_body, tokens, blocks, nstate, taps),
        out_shape=[vec(r) for r in [full] * 4 + [edge, splats, splats, rated]],
        in_specs=[hbm] * 4 + [vmem] * 4 + [hbm],
        out_specs=[vmem] * 8,
        scratch_shapes=[
            pltpu.VMEM((4, tokens, channels), jnp.bfloat16), pltpu.SemaphoreType.DMA((4,)),
        ],
        compiler_params=limit(LOCAL_MB),
        cost_estimate=cost(3, full * LANE * 8),
        name="prepare",
    )(
        *far(xin, delta_raw, zgate, grad_out, bmat, cmat, dtb, decay_rate), rate_mine
    )
    pay, skipped, dus, us, sls, xs = pl.pallas_call(
        functools.partial(local_body, tokens, blocks, nstate, taps),
        out_shape=[f32(blocks * wide, LANE), f32(blocks, LANE)]
        + [vec(r) for r in [full] * 3 + [edge]],
        in_specs=[vmem] * 9,
        out_specs=[vmem] * 6,
        scratch_shapes=[vec(taps * blocks)],
        input_output_aliases={8: 5},
        compiler_params=limit(LOCAL_MB),
        cost_estimate=cost(9, full * LANE * 36),
        name="local_scan",
    )(rim, *far(conv_w, cb), dts, gys, bs, cs, nrates, xs)
    factors = (dts, dus, gys, us, zfs, sls, sds, xs, bs, cs, nrates)
    got = swap(slices(pay.reshape(blocks, wide, LANE), runs))
    carries = pl.pallas_call(
        functools.partial(carry_body, runs, mine, span, nstate, wide),
        out_shape=f32(runs * mine * 2 * nstate, span),
        in_specs=[vmem] * 2,
        out_specs=vmem,
        compiler_params=limit(CARRY_MB),
        name="carry_scan",
    )(got.reshape(runs * mine * wide, span), rate_mine)
    ins = unslices(swap(carries.reshape(runs, mine * 2 * nstate, span)), blocks, 2 * nstate)
    rows = nstate + taps + 3
    rows = rows + (-rows) % SUB
    away = lambda rows: pltpu.HBM((rows, LANE), jnp.float32)
    dcv, gz, dd, gb, gc, par = pl.pallas_call(
        functools.partial(grads_body, tokens, blocks, nstate, taps),
        out_shape=(*[away(full)] * 3, *[away(splats * SUB)] * 2, f32(blocks * rows, LANE)),
        in_specs=[vmem] * 14,
        out_specs=(*[hbm] * 5, vmem),
        scratch_shapes=[
            vec(full), vec(full), vec(full), vec((tokens + 1) * GROUP * blocks),
            vec(splats * SUB), vec(splats * SUB), pltpu.SemaphoreType.DMA((blocks // SUB, 3)),
            pltpu.SemaphoreType.DMA((2, nstate // GROUP)),
        ],
        compiler_params=limit(GRADS_MB),
        cost_estimate=cost(22, nstate * full * LANE),
        name="grads",
    )(ins.reshape(blocks * 2 * nstate, LANE), *far(skip), skipped, *factors)
    summed = swap(slices(par.reshape(blocks, rows, LANE), runs))
    gx, gz, gd, gc, owed = pl.pallas_call(
        functools.partial(outs_body, tokens, blocks, taps),
        out_shape=(
            *[pltpu.HBM((tokens, channels), jnp.bfloat16)] * 3, away(splats),
            f32(2 * lead, blocks, LANE),
        ),
        in_specs=[vmem] + [hbm] * 4,
        out_specs=tuple([vmem] * 5),
        scratch_shapes=[
            vec(full), vec(full), vec(full), vec(splats * SUB), vec(full), vec(taps * blocks),
            pltpu.SemaphoreType.DMA((4,)),
        ],
        compiler_params=limit(GRADS_MB),
        cost_estimate=pl.CostEstimate(
            flops=8 * full * LANE, bytes_accessed=5 * full * LANE * 4, transcendentals=0
        ),
        name="outs",
    )(*far(conv_w, dcv, gz, dd, gc))
    sums = jnp.sum(summed, axis=0)
    sums, owed = lax.optimization_barrier((sums, owed))
    gb = jnp.sum(gb.reshape(nstate, tokens, SUB, LANE), axis=(2, 3))
    gc = jnp.sum(gc.reshape(nstate, tokens, LANE), axis=2)
    returned = lax.ppermute(owed[:lead], "seq", [(i + 1, i) for i in range(runs - 1)])
    last = (owed[lead:] + returned).reshape(lead, channels).astype(jnp.bfloat16)
    gx = lax.dynamic_update_slice(gx, last, (tokens - lead, 0))
    every = unslices(swap(jnp.broadcast_to(sums[None], (runs,) + sums.shape)), blocks, rows)
    convw, rate, *lines = pl.pallas_call(
        functools.partial(finish_body, blocks, nstate, taps),
        out_shape=[f32(taps, channels), f32(nstate, channels)] + [f32(blocks, LANE)] * 3,
        in_specs=[vmem],
        out_specs=[vmem] * 5,
        compiler_params=limit(CARRY_MB),
        name="finish",
    )(every.reshape(blocks * rows, LANE))
    convb, skips, bias = (v.reshape(channels) for v in lines)
    return gx, gz, gd, gb, gc, convw, convb, rate, skips, bias


def solution(mesh):
    both = P(("dp", "seq"), None)
    across = P(None, ("dp", "seq"))
    return jax.shard_map(
        shards,
        mesh=mesh,
        in_specs=(both, both, both, across, across, P(), P(), P(), P(), P(), both),
        out_specs=(
            both, both, both, across, across,
            P("dp", None), P("dp"), P("dp", None), P("dp"), P("dp"),
        ),
        check_vma=False,
    )
```
